32 devices in a mesh: body: 2 (over y), row: 4 (over z), sub: 4 (over x, core).
Axes of the slice: x: 2, y: 2, z: 4, core: 2. Of those that a mesh axis runs over, the one named last changes fastest.
Arguments:
- positions: float32 [8, 3, 10240], P(('body', 'sub'), None, 'row'), parts along dimension 0, may hold values from 0 to 1
- panel_area: float32 [8, 10240], P(('body', 'sub'), 'row'), parts along dimension 0, may hold values from 0.3 to 3
- self_term: float32 [8, 10240], P(('body', 'sub'), 'row'), parts along dimension 0, may hold values from 3 to 8
- excitation: float32 [8, 8, 10240], P(('body', 'sub'), None, 'row'), parts along dimension 0, may hold values from -6 to 6
- adjacency: int32 [8, 2], P('body'), parts along dimension 0, may hold values from 0 to 3, as said below
- block_list: int32 [8, 2, 32], P('body'), parts along dimension 0, may hold values from 0 to 319, as said below
- block_count: int32 [8, 2], P('body'), parts along dimension 0, may hold values from 1 to 32, as said below
Outputs:
- currents: float32 [8, 8, 10240], P(('body', 'sub'), None, 'row'), parts along dimension 0
- residual: float32 [8, 8, 10240], P(('body', 'sub'), None, 'row'), parts along dimension 0
The draws below stay inside these ranges and needn't reach their ends.
There are 2 independent parts, one for each index of `body`. The reference program is written for one: setup_inputs(seed, part) draws one part's arguments, and reference() takes and returns one part's arrays. A program takes and returns all parts, laid end to end along the dimension named above; each array names one. Nothing has to cross between parts.
Inputs may be any that keep to these rules, and one draw needn't show every extreme that they name: `adjacency`: each subdomain lists 2 different subdomains other than itself. `block_list`: in each pair the first block_count entries are different; later entries are not used. `block_count`: some pair has exactly 32 blocks.
All inputs are finite; a program needn't handle non-finite values.
Results may differ from the reference program's by a relative error of at most 0.0003.
Values sent between devices are 32-bit elements; how exact they have to be, the bound alone decides.
No kernel may reach another device: no remote copies, remote signals or barrier semaphores. Data moves between devices by JAX's collectives and lax.ppermute only.
A program may use at most 192 MiB of HBM per device.

```python
import math
import jax
import jax.numpy as jnp
from jax import lax

NU = 10240
E = 8
BLK = 32
NADJ = 2
MAXB = 32
OUTER = 2
INNER = 2
SUBS = 4
NBLK = 320


def draw_links(key):
    key_adj = jax.random.fold_in(key, 101)
    key_blk = jax.random.fold_in(key, 102)
    key_cnt = jax.random.fold_in(key, 103)
    key_top = jax.random.fold_in(key, 104)
    scores = jax.random.randint(key_adj, (SUBS, SUBS), 0, 1000) * SUBS + jnp.arange(SUBS, dtype=jnp.int32)[None, :]
    scores = scores + jnp.eye(SUBS, dtype=jnp.int32) * (1001 * SUBS)
    ranking = jnp.argsort(scores, axis=1, stable=True)
    adjacency = ranking[:, :NADJ].astype(jnp.int32)
    block_scores = jax.random.randint(key_blk, (SUBS, NADJ, NBLK), 0, 1 << 20) * NBLK + jnp.arange(NBLK, dtype=jnp.int32)
    blocks = jnp.argsort(block_scores, axis=2, stable=True)[:, :, :MAXB].astype(jnp.int32)
    counts = jax.random.randint(key_cnt, (SUBS * NADJ,), 1, MAXB + 1)
    chosen = jax.random.randint(key_top, (), 0, SUBS * NADJ)
    counts = jnp.where(jnp.arange(SUBS * NADJ, dtype=jnp.int32) == chosen, MAXB, counts)
    return (adjacency, blocks, counts.reshape(SUBS, NADJ).astype(jnp.int32))


def draw_adjacency(key, part):
    return draw_links(key)[0]


def draw_block_list(key, part):
    return draw_links(key)[1]


def draw_block_count(key, part):
    return draw_links(key)[2]


def steps_of(stream_key, extent, cuts, low, largest):
    level = 1.0
    for axis_at, parts in cuts:
        heights = jax.random.uniform(jax.random.fold_in(jax.random.fold_in(stream_key, 6), axis_at), (parts,), jnp.float32, low / len(cuts), largest / len(cuts))
        level = level * jnp.repeat(jnp.exp(heights), extent[axis_at] // parts).reshape((-1,) + (1,) * (len(extent) - 1 - axis_at))
    return level


def noise(stream_key, shape, scale, limit, split=(), kind=jnp.bfloat16):
    loudness = steps_of(stream_key, shape, split, -0.22, 0.18) if split else 1.0
    drawn = jax.random.normal(stream_key, shape, jnp.float32) * scale * loudness
    return jnp.minimum(jnp.maximum(drawn, -limit), limit).astype(kind)


def setup_inputs(seed: int = 0, part: int = 0) -> dict:
    streams_of = jax.random.split(jax.random.key(seed), 8)
    part_keys = jax.random.split(jax.random.fold_in(streams_of[7], part), 8)
    positions = jnp.clip(1.0 * jax.random.uniform(part_keys[0], (SUBS, 3, NU), jnp.float32) ** steps_of(part_keys[0], (SUBS, 3, NU), ((0, 4), (2, 4)), -0.2, 0.2), 0.0, 1.0)
    panel_area = jnp.clip(jnp.exp(math.log(3.0) - 2.3025851 * jax.random.uniform(part_keys[1], (SUBS, NU), jnp.float32) ** steps_of(part_keys[1], (SUBS, NU), ((0, 4), (1, 4)), -0.2, 0.2)), 0.3, 3.0)
    self_term = jnp.clip(jnp.exp(math.log(8.0) - 0.98082925 * jax.random.uniform(part_keys[2], (SUBS, NU), jnp.float32) ** steps_of(part_keys[2], (SUBS, NU), ((0, 4), (1, 4)), -0.2, 0.2)), 3.0, 8.0)
    excitation = noise(part_keys[3], (SUBS, E, NU), 1.0, 6.0, ((0, 4), (2, 4)), jnp.float32)
    adjacency = draw_adjacency(jax.random.fold_in(jax.random.fold_in(streams_of[7], part), 71), part)
    block_list = draw_block_list(jax.random.fold_in(jax.random.fold_in(streams_of[7], part), 71), part)
    block_count = draw_block_count(jax.random.fold_in(jax.random.fold_in(streams_of[7], part), 71), part)
    return {"positions": positions, "panel_area": panel_area, "self_term": self_term, "excitation": excitation, "adjacency": adjacency, "block_list": block_list, "block_count": block_count}


KAPPA = 40.0
COUPLE = 1.0
EPS = 1e-06
row_block = 2048

def kernel_tile(near, far, area, scale):
    squared = jnp.zeros(near.shape[1:] + far.shape[-1:], jnp.float32)
    for coord in range(3):
        spacing = near[coord][..., :, None] - far[coord][..., None, :]
        squared = squared + spacing * spacing
    radius = jnp.sqrt(squared)
    return jnp.cos(KAPPA * radius) / (1.0 + radius) * (area * scale)[..., None, :]

def apply_self(points, weights, diagonal, field):
    scale = 1.0 / math.sqrt(NU)
    starts = jnp.arange(NU // row_block, dtype=jnp.int32) * row_block

    def one_block(start):
        near = lax.dynamic_slice_in_dim(points, start, row_block, 1)
        tile = kernel_tile(near, points, weights, scale)
        return lax.dot_general(field, tile, (((1,), (1,)), ((), ())), precision=lax.Precision.HIGHEST, preferred_element_type=jnp.float32)
    pieces = lax.map(one_block, starts)
    product = jnp.transpose(pieces, (1, 0, 2)).reshape(field.shape[0], NU)
    return diagonal[None, :] * field + product

def couple(positions, panel_area, currents, adjacency, block_list, block_count):
    width = currents.shape[1]
    results = []
    for target in range(SUBS):
        total = jnp.zeros((width, NBLK, BLK), jnp.float32)
        for slot in range(NADJ):
            source = adjacency[target, slot].astype(jnp.int32)
            src_pos = lax.dynamic_index_in_dim(positions, source, 0, keepdims=False)
            src_area = lax.dynamic_index_in_dim(panel_area, source, 0, keepdims=False)
            src_cur = lax.dynamic_index_in_dim(currents, source, 0, keepdims=False)
            tiles = kernel_tile(positions[target].reshape(3, NBLK, BLK), src_pos.reshape(3, NBLK, BLK), src_area.reshape(NBLK, BLK), COUPLE / math.sqrt(BLK))
            product = jnp.einsum('bpq,ebq->ebp', tiles, src_cur.reshape(width, NBLK, BLK), precision=lax.Precision.HIGHEST)
            listed = (block_list[target, slot][:, None] == jnp.arange(NBLK, dtype=jnp.int32)[None, :]) & (jnp.arange(MAXB, dtype=jnp.int32)[:, None] < block_count[target, slot])
            weight = lax.optimization_barrier(jnp.sum(listed.astype(jnp.float32), axis=0))
            total = total + product * weight[None, :, None]
        results.append(total.reshape(width, NU))
    return jnp.stack(results)

def reference(positions, panel_area, self_term, excitation, adjacency, block_list, block_count):
    currents = jnp.zeros_like(excitation)
    residual = excitation
    previous = jnp.zeros_like(excitation)
    for outer_step in range(OUTER):
        if outer_step > 0:
            coupled = couple(positions, panel_area, currents, adjacency, block_list, block_count)
            residual = residual - (coupled - previous)
            previous = coupled
        for inner_step in range(INNER):
            image = jnp.stack([apply_self(positions[target], panel_area[target], self_term[target], residual[target]) for target in range(SUBS)])
            alpha = lax.optimization_barrier(jnp.sum(residual * image, axis=2)) / (lax.optimization_barrier(jnp.sum(image * image, axis=2)) + EPS)
            currents = currents + alpha[:, :, None] * residual
            residual = residual - alpha[:, :, None] * image
    return (currents, residual)
```

```python
import functools
import math

import jax
import jax.numpy as jnp
from jax import lax
from jax.experimental import pallas as pl
from jax.experimental.pallas import tpu as pltpu
from jax.sharding import PartitionSpec as P

BLK = 32
OUTER = 2

KAPPA = 40.0
COUPLE = 1.0
EPS = 1e-06
column_block = 2048

F32 = jnp.float32
BF16 = jnp.bfloat16
TILE = 256
CHUNK = 32
FEATURES = 96
WAVE = KAPPA / (2.0 * math.pi)
ROUNDER = 12582912.0
COSINE = (
    0.999999210782322,
    -19.738980355764046,
    64.92865742103419,
    -85.27162153430582,
    58.790492120148535,
    -21.07110562765538,
)


def to_grid(x, step):
    shift = ROUNDER * step
    return (x + shift) - shift


def cos_turns(turns):
    u = turns - to_grid(turns, 1.0)
    s = u * u
    value = jnp.full_like(s, COSINE[-1])
    for coefficient in COSINE[-2::-1]:
        value = value * s + coefficient
    return value


def green(squared_turns):
    y = jnp.maximum(squared_turns, 1e-12)
    turns = y * lax.rsqrt(y)
    u = turns - to_grid(turns, 1.0)
    s = u * u
    value = COSINE[-1] * WAVE
    for coefficient in COSINE[-2::-1]:
        value = value * s + coefficient * WAVE
    return value / (turns + WAVE)


def features(points):
    row = lax.broadcasted_iota(jnp.int32, points.shape, 0)
    centred = jnp.where(row < 3, (points - 0.5) * WAVE, 0.0)
    high = to_grid(centred, 2.0**-6)
    rest = centred - high
    mid = to_grid(rest, 2.0**-14)
    low = rest - mid
    coarse = jnp.sum(high * high, axis=0, keepdims=True)
    fine = jnp.sum(2.0 * high * rest + rest * rest, axis=0, keepdims=True)
    a = to_grid(coarse, 0.25)
    b = to_grid(coarse - a, 2.0**-10)
    c = coarse - a - b
    d = fine.astype(BF16).astype(F32)
    e = (fine - d).astype(BF16).astype(F32)
    f = fine - d - e
    norm = jnp.zeros_like(centred)
    for k, piece in enumerate((a, b, c, d, e, f)):
        norm = jnp.where(row == k, piece, norm)
    one = jnp.where(row < 6, 1.0, 0.0)
    zero = jnp.zeros_like(centred)
    left = (high, norm, one, high, mid, high, low, mid, mid, low, low, zero)
    right = (high, one, norm, mid, high, low, high, mid, low, mid, low, zero)
    right = tuple(-2.0 * x if k not in (1, 2) else x for k, x in enumerate(right))
    return left, right


def two_pieces(x):
    high = x.astype(BF16).astype(F32)
    return jnp.concatenate([high, x - high], axis=0).astype(BF16)


def nn(left, right):
    return lax.dot_general(left, right, (((1,), (0,)), ((), ())), preferred_element_type=F32)


def nt(left, right):
    return lax.dot_general(left, right, (((1,), (1,)), ((), ())), preferred_element_type=F32)


def prep_kernel(scale, doubled, pack_ref, left_ref, right_ref, field_ref):
    pack = pack_ref[...]
    count = pack.shape[1]
    left, right = features(pack[:8])
    right = jnp.concatenate(right, axis=0).astype(BF16)
    field = two_pieces(pack[8:] * (pack[3:4] * scale))
    if doubled:
        for k in range(2):
            right_ref[:, k * count : (k + 1) * count] = right
            field_ref[:, k * count : (k + 1) * count] = field
        left = jnp.concatenate(left + (jnp.zeros((128 - FEATURES, count), F32),), axis=0)
        for k in range(count // TILE):
            left_ref[k * TILE : (k + 1) * TILE, :] = left[:, k * TILE : (k + 1) * TILE].T.astype(BF16)
    else:
        half = count // 2
        for k in range(count // TILE):
            to = (k % 2) * half + (k // 2) * TILE
            right_ref[:, to : to + TILE] = right[:, k * TILE : (k + 1) * TILE]
            field_ref[:, to : to + TILE] = field[:, k * TILE : (k + 1) * TILE]


def fill_tile(source, at, target_high, target_low, to):
    for c in range(TILE // CHUNK):
        rows = slice(c * CHUNK, (c + 1) * CHUNK)
        g = green(source[rows, at : at + TILE])
        high = g.astype(BF16)
        target_high[rows, to : to + TILE] = high
        target_low[rows, to : to + TILE] = (g - high.astype(F32)).astype(BF16)


def build_own_kernel(left_ref, right_ref, field_ref, high_ref, low_ref, acc_ref, dist):
    i = pl.program_id(0)
    width = high_ref.shape[1]
    tiles = width // TILE
    here = pl.multiple_of(i * TILE, TILE)

    @pl.when(i == 0)
    def _():
        acc_ref[...] = jnp.zeros_like(acc_ref)

    dist[...] = nn(
        left_ref[pl.ds(here, TILE), :FEATURES], right_ref[:, pl.ds(here, width)]
    )
    mine = field_ref[:, pl.ds(here, TILE)]
    total = jnp.zeros((16, TILE), F32)
    for k in range(tiles):
        fill_tile(dist, k * TILE, high_ref, low_ref, k * TILE)
        there = pl.ds(pl.multiple_of(here + k * TILE, TILE), TILE)
        high = high_ref[:, k * TILE : (k + 1) * TILE]
        low = low_ref[:, k * TILE : (k + 1) * TILE]
        other = field_ref[:, there]
        total = total + nt(other, high) + nt(other, low)
        if 0 < k < tiles - 1:
            acc_ref[:, there] += nn(mine, high) + nn(mine, low)
    acc_ref[:, pl.ds(here, TILE)] += total


def fold_pieces(x):
    return x[:8] + x[8:]


def write_partial(part_ref, acc_own, acc_oth):
    count = acc_own.shape[1] // 2
    half = count // 2
    part_ref[:, :count] = fold_pieces(acc_own[:, :count] + acc_own[:, count:])
    for b in range(3):
        for k in range(count // TILE):
            at = b * count + (k % 2) * half + (k // 2) * TILE
            to = (b + 1) * count + k * TILE
            part_ref[:, to : to + TILE] = fold_pieces(acc_oth[:, at : at + TILE])


def build_oth_kernel(
    parity_ref, left_ref, right_ref, own_ref, field_ref, acc_in_ref,
    high_ref, low_ref, part_ref, dist, acc_own, acc_oth,
):
    i = pl.program_id(0)
    count = left_ref.shape[0]
    half = count // 2
    tiles = half // TILE
    here = pl.multiple_of(i * TILE, TILE)

    @pl.when(i == 0)
    def _():
        acc_own[...] = acc_in_ref[...]
        acc_oth[...] = jnp.zeros_like(acc_oth)

    offsets = [
        pl.multiple_of(b * count + ((i + parity_ref[b]) & 1) * half, TILE) for b in range(3)
    ]
    left = left_ref[pl.ds(here, TILE), :FEATURES]
    mine = own_ref[:, pl.ds(here, TILE)]
    total = jnp.zeros((16, TILE), F32)
    dist[0] = nn(left, right_ref[:, pl.ds(offsets[0], half)])
    for b in range(3):
        if b < 2:
            dist[(b + 1) % 2] = nn(left, right_ref[:, pl.ds(offsets[b + 1], half)])
        for k in range(tiles):
            to = b * half + k * TILE
            fill_tile(dist.at[b % 2], k * TILE, high_ref, low_ref, to)
            there = pl.ds(pl.multiple_of(offsets[b] + k * TILE, TILE), TILE)
            high = high_ref[:, to : to + TILE]
            low = low_ref[:, to : to + TILE]
            other = field_ref[:, there]
            total = total + nt(other, high) + nt(other, low)
            acc_oth[:, there] += nn(mine, high) + nn(mine, low)
    acc_own[:, pl.ds(here, TILE)] += total

    @pl.when(i == pl.num_programs(0) - 1)
    def _():
        write_partial(part_ref, acc_own, acc_oth)


def mr_step(even_ref, odd_ref, pack_ref, res_ref, cur_ref, new_res_ref, new_cur_ref):
    count = even_ref.shape[1] // 2
    image = []
    numerator = 0.0
    denominator = 0.0
    for b in range(4):
        source = odd_ref if b % 2 else even_ref
        product = source[:, (b // 2) * count : (b // 2 + 1) * count]
        cols = slice(b * count, (b + 1) * count)
        res = res_ref[:, cols]
        img = pack_ref[4:5, cols] * res + product
        new_res_ref[:, cols] = img
        numerator = numerator + jnp.sum(res * img, axis=1, keepdims=True)
        denominator = denominator + jnp.sum(img * img, axis=1, keepdims=True)
    alpha = numerator / (denominator + EPS)
    for b in range(4):
        cols = slice(b * count, (b + 1) * count)
        res = res_ref[:, cols]
        if cur_ref is None:
            new_cur_ref[:, cols] = alpha * res
        else:
            new_cur_ref[:, cols] = cur_ref[:, cols] + alpha * res
        new_res_ref[:, cols] = res - alpha * new_res_ref[:, cols]


def step_kernel(even_ref, odd_ref, pack_ref, res_ref, cur_ref, new_res_ref, new_cur_ref):
    mr_step(even_ref, odd_ref, pack_ref, res_ref, cur_ref, new_res_ref, new_cur_ref)


def apply_kernel(scale, first, with_low, couple, *refs):
    refs = list(refs)
    parity_ref = refs.pop(0)
    even_ref, odd_ref, pack_ref, res_ref = refs[:4]
    refs = refs[4:]
    cur_ref = None if first or couple else refs.pop(0)
    own_high, oth_high = refs[:2]
    refs = refs[2:]
    pieces = [(own_high, oth_high)]
    if with_low:
        pieces.append((refs[0], refs[1]))
        refs = refs[2:]
    new_res_ref = refs.pop(0)
    new_cur_ref = None if couple else refs.pop(0)
    part_ref, own_field, oth_field, acc_own, acc_oth = refs

    i = pl.program_id(0)
    count = even_ref.shape[1] // 2
    half = count // 2
    here = pl.multiple_of(i * TILE, TILE)

    @pl.when(i == 0)
    def _():
        acc_own[...] = jnp.zeros_like(acc_own)
        acc_oth[...] = jnp.zeros_like(acc_oth)
        if couple:
            for b in range(4):
                source = odd_ref if b % 2 else even_ref
                cols = slice(b * count, (b + 1) * count)
                new_res_ref[:, cols] = (
                    res_ref[:, cols] - source[:, (b // 2) * count : (b // 2 + 1) * count]
                )
        else:
            mr_step(even_ref, odd_ref, pack_ref, res_ref, cur_ref, new_res_ref, new_cur_ref)
        for b in range(4):
            for k in range(count // TILE):
                cols = slice(b * count + k * TILE, b * count + (k + 1) * TILE)
                field = two_pieces(new_res_ref[:, cols] * (pack_ref[3:4, cols] * scale))
                if b == 0:
                    own_field[:, k * TILE : (k + 1) * TILE] = field
                    own_field[:, count + k * TILE : count + (k + 1) * TILE] = field
                else:
                    to = (b - 1) * count + (k % 2) * half + (k // 2) * TILE
                    oth_field[:, to : to + TILE] = field

    width = own_high.shape[1]
    mine = own_field[:, pl.ds(here, TILE)]
    span = pl.ds(here, width)
    inner = pl.ds(pl.multiple_of(here + TILE, TILE), width - 2 * TILE)
    total = jnp.zeros((16, TILE), F32)
    for own_ref, _ in pieces:
        total = total + nt(own_field[:, span], own_ref[...])
        acc_own[:, inner] += nn(mine, own_ref[:, TILE : width - TILE])
    for b in range(3):
        there = pl.ds(
            pl.multiple_of(b * count + ((i + parity_ref[b]) & 1) * half, TILE), half
        )
        for _, oth_ref in pieces:
            block = oth_ref[:, b * half : (b + 1) * half]
            total = total + nt(oth_field[:, there], block)
            acc_oth[:, there] += nn(mine, block)
    acc_own[:, pl.ds(here, TILE)] += total

    @pl.when(i == pl.num_programs(0) - 1)
    def _():
        write_partial(part_ref, acc_own, acc_oth)


def couple_kernel(source_ref, list_ref, count_ref, first_ref, near_ref, far_ref, cur_ref, out_ref):
    count = near_ref.shape[1]
    lane = lax.broadcasted_iota(jnp.int32, (1, count), 1)
    ident = first_ref[0] + lane // BLK
    row = lax.broadcasted_iota(jnp.int32, (128, 128), 0) // BLK
    col = lax.broadcasted_iota(jnp.int32, (128, 128), 1) // BLK
    same = row == col
    total = None
    weights = []
    for slot in range(count_ref.shape[0]):
        hits = jnp.zeros((1, count), F32)
        for k in range(list_ref.shape[1]):
            hit = (ident == list_ref[slot, k]) & (k < count_ref[slot])
            hits = hits + jnp.where(hit, 1.0, 0.0)
        weights.append(hits)
    for g in range(count // 128):
        cols = slice(g * 128, (g + 1) * 128)
        near = near_ref[:8, cols].T
        total = jnp.zeros((8, 128), F32)
        for slot in range(count_ref.shape[0]):
            far = far_ref[source_ref[slot], :, cols]
            squared = jnp.zeros((128, 128), F32)
            for x in range(3):
                gap = near[:, x : x + 1] - far[x : x + 1, :]
                squared = squared + gap * gap
            safe = jnp.maximum(squared, 1e-30)
            radius = safe * lax.rsqrt(safe)
            tile = cos_turns(radius * WAVE) / (1.0 + radius)
            tile = jnp.where(same, tile, 0.0)
            field = cur_ref[source_ref[slot], :, cols] * (far[3:4, :] * (COUPLE / math.sqrt(BLK)))
            high = tile.astype(BF16)
            low = (tile - high.astype(F32)).astype(BF16)
            pieces = two_pieces(field)
            product = nt(pieces, high) + nt(pieces, low)
            total = total + fold_pieces(product) * weights[slot][:, cols]
        out_ref[:, cols] = total


def whole(shape):
    return pl.BlockSpec(shape, lambda i, *_: (0,) * len(shape))


SMEM = pl.BlockSpec(memory_space=pltpu.SMEM)
VMEM_LIMIT = 48 * 1024 * 1024


def params(**kw):
    return pltpu.CompilerParams(vmem_limit_bytes=VMEM_LIMIT, **kw)


def on_plane(positions, panel_area, self_term, excitation, adjacency, block_list, block_count):
    count = excitation.shape[2]
    subs = adjacency.shape[0]
    ranks = subs
    unknowns = count * ranks
    scale = 1.0 / math.sqrt(unknowns)
    tiles = count // TILE
    half = count // 2
    own_width = (tiles // 2 + 1) * TILE
    plane = lax.axis_index("row")
    place = lax.axis_index("sub")

    swap = [(z * subs + s, s * subs + z) for z in range(ranks) for s in range(subs)]

    def over(bit):
        return [(s, s ^ bit) for s in range(subs)]

    def send(x, bit):
        return lax.ppermute(x, "sub", over(bit))

    pack = jnp.concatenate(
        [
            positions[0],
            panel_area,
            self_term,
            jnp.zeros((3, count), F32),
            excitation[0],
        ],
        axis=0,
    )
    pack = lax.ppermute(pack, ("row", "sub"), swap)

    f32 = lambda *s: jax.ShapeDtypeStruct(s, F32)
    b16 = lambda *s: jax.ShapeDtypeStruct(s, BF16)

    left, right_own, field_own = pl.pallas_call(
        functools.partial(prep_kernel, scale, True),
        out_shape=(b16(count, 128), b16(FEATURES, 2 * count), b16(16, 2 * count)),
        compiler_params=params(),
        name="prep_own",
    )(pack)

    pack2 = send(pack, 2)
    packs = jnp.stack([pack, pack2])
    packs_odd = send(packs, 1)
    full = jnp.concatenate([pack, packs_odd[0], pack2, packs_odd[1]], axis=1)

    own_high, own_low, acc = pl.pallas_call(
        build_own_kernel,
        grid=(tiles,),
        in_specs=[
            whole((count, 128)),
            whole((FEATURES, 2 * count)),
            whole((16, 2 * count)),
        ],
        out_specs=(
            pl.BlockSpec((TILE, own_width), lambda i: (i, 0)),
            pl.BlockSpec((TILE, own_width), lambda i: (i, 0)),
            whole((16, 2 * count)),
        ),
        out_shape=(b16(count, own_width), b16(count, own_width), f32(16, 2 * count)),
        scratch_shapes=[pltpu.VMEM((TILE, own_width), F32)],
        compiler_params=params(),
        cost_estimate=pl.CostEstimate(
            flops=60 * count * own_width, bytes_accessed=4 * count * own_width, transcendentals=0
        ),
        name="build_own",
    )(left, right_own, field_own)

    right_oth, field_oth = [], []
    for b in range(1, 4):
        r, f = pl.pallas_call(
            lambda p, r, f: prep_kernel(scale, False, p, None, r, f),
            out_shape=(b16(FEATURES, count), b16(16, count)),
            compiler_params=params(),
            name="prep_oth",
        )(full[:, b * count : (b + 1) * count])
        right_oth.append(r)
        field_oth.append(f)
    right_oth = jnp.concatenate(right_oth, axis=1)
    field_oth = jnp.concatenate(field_oth, axis=1)

    parity = jnp.stack([(place > (place ^ b)).astype(jnp.int32) for b in range(1, 4)])

    oth_high, oth_low, part = pl.pallas_call(
        build_oth_kernel,
        grid_spec=pltpu.PrefetchScalarGridSpec(
            num_scalar_prefetch=1,
            grid=(tiles,),
            in_specs=[
                whole((count, 128)),
                whole((FEATURES, 3 * count)),
                whole((16, 2 * count)),
                whole((16, 3 * count)),
                whole((16, 2 * count)),
            ],
            out_specs=(
                pl.BlockSpec((TILE, 3 * half), lambda i, *_: (i, 0)),
                pl.BlockSpec((TILE, 3 * half), lambda i, *_: (i, 0)),
                whole((8, 4 * count)),
            ),
            scratch_shapes=[
                pltpu.VMEM((2, TILE, half), F32),
                pltpu.VMEM((16, 2 * count), F32),
                pltpu.VMEM((16, 3 * count), F32),
            ],
        ),
        out_shape=(b16(count, 3 * half), b16(count, 3 * half), f32(8, 4 * count)),
        compiler_params=params(),
        name="build_oth",
    )(parity, left, right_oth, field_own, field_oth, acc)

    def pair(x, a, b):
        return jnp.concatenate(
            [x[:, a * count : (a + 1) * count], x[:, b * count : (b + 1) * count]], axis=1
        )

    def reduce_all(part):
        got = send(pair(part, 1, 3), 1)
        chip = pair(part, 0, 2) + got
        got = send(chip, 2)
        even = chip + pair(got, 1, 0)
        odd = send(even, 1)
        return even, odd

    def apply(even, odd, res, cur, with_low, couple):
        first = cur is None and not couple
        operands = [even, odd, full, res]
        specs = [
            whole((8, 2 * count)),
            whole((8, 2 * count)),
            whole((16, 4 * count)),
            whole((8, 4 * count)),
        ]
        if not first and not couple:
            operands.append(cur)
            specs.append(whole((8, 4 * count)))
        own_spec = pl.BlockSpec((TILE, own_width), lambda i, *_: (i, 0))
        oth_spec = pl.BlockSpec((TILE, 3 * half), lambda i, *_: (i, 0))
        operands += [own_high, oth_high]
        specs += [own_spec, oth_spec]
        if with_low:
            operands += [own_low, oth_low]
            specs += [own_spec, oth_spec]
        outs = 2 if couple else 3
        return pl.pallas_call(
            functools.partial(apply_kernel, scale, first, with_low, couple),
            grid_spec=pltpu.PrefetchScalarGridSpec(
                num_scalar_prefetch=1,
                grid=(tiles,),
                in_specs=specs,
                out_specs=[whole((8, 4 * count))] * outs,
                scratch_shapes=[
                    pltpu.VMEM((16, 2 * count), BF16),
                    pltpu.VMEM((16, 3 * count), BF16),
                    pltpu.VMEM((16, 2 * count), F32),
                    pltpu.VMEM((16, 3 * count), F32),
                ],
            ),
            out_shape=[f32(8, 4 * count)] * outs,
            compiler_params=params(),
            name="apply",
        )(parity, *operands)

    even, odd = reduce_all(part)
    res, cur, part = apply(even, odd, full[8:], None, True, False)
    even, odd = reduce_all(part)
    res, cur = pl.pallas_call(
        step_kernel,
        out_shape=[f32(8, 4 * count)] * 2,
        compiler_params=params(),
        name="step",
    )(even, odd, full, res, cur)

    def from_planes(x):
        return jnp.stack(
            [
                lax.ppermute(x, "row", [(z, (z + k) % ranks) for z in range(ranks)])
                for k in range(1, ranks)
            ]
        )

    far = from_planes(pack[:8])
    far_cur = from_planes(cur[:, :count])
    mine = jnp.arange(subs, dtype=jnp.int32) == plane
    neighbours = jnp.sum(jnp.where(mine[:, None], adjacency, 0), axis=0)
    lists = jnp.sum(jnp.where(mine[:, None, None], block_list, 0), axis=0)
    counts = jnp.sum(jnp.where(mine[:, None], block_count, 0), axis=0)
    source = (plane - neighbours + subs) % subs - 1
    first_block = (place * (count // BLK)).astype(jnp.int32).reshape(1)
    coupled = pl.pallas_call(
        couple_kernel,
        in_specs=[SMEM] * 4 + [pl.BlockSpec(memory_space=pltpu.VMEM)] * 3,
        out_shape=f32(8, count),
        compiler_params=params(),
        name="couple",
    )(source, lists, counts, first_block, pack, far, far_cur)
    even = jnp.concatenate([coupled, send(coupled, 2)], axis=1)
    odd = send(even, 1)

    res, part = apply(even, odd, res, None, True, True)
    even, odd = reduce_all(part)
    res, cur, part = apply(even, odd, res, cur, True, False)
    even, odd = reduce_all(part)
    res, cur = pl.pallas_call(
        step_kernel,
        out_shape=[f32(8, 4 * count)] * 2,
        compiler_params=params(),
        name="step",
    )(even, odd, full, res, cur)
    out = jnp.concatenate([cur[:, :count], res[:, :count]], axis=0)
    out = lax.ppermute(out, ("row", "sub"), swap)
    return out[None, :8], out[None, 8:]


def kernel_tile(near, far, area, scale):
    squared = jnp.zeros(near.shape[1:] + far.shape[-1:], jnp.float32)
    for coord in range(3):
        spacing = near[coord][..., :, None] - far[coord][..., None, :]
        squared = squared + spacing * spacing
    radius = jnp.sqrt(squared)
    return jnp.cos(KAPPA * radius) / (1.0 + radius) * (area * scale)[..., None, :]


def pick_source(table, chosen):
    shaped = chosen.reshape(chosen.shape + (1,) * (table.ndim - 1))
    return jnp.sum(jnp.where(shaped, table, jnp.zeros_like(table)), axis=0)


def on_rows(positions, panel_area, self_term, excitation, adjacency, block_list, block_count):
    width = excitation.shape[1]
    rows_here = excitation.shape[2]
    near = positions[0]
    diagonal = self_term[0]
    gathered_pos, gathered_area = (
        lax.all_gather(positions[0], "row", axis=1, tiled=True),
        lax.all_gather(panel_area[0], "row", axis=0, tiled=True),
    )
    other_pos, other_area = (
        lax.all_gather(positions, "sub", axis=0, tiled=True),
        lax.all_gather(panel_area, "sub", axis=0, tiled=True),
    )
    total_cols = gathered_pos.shape[1]
    scale = 1.0 / math.sqrt(total_cols)
    subdomains = adjacency.shape[0]
    local_blocks = rows_here // BLK

    def build_step(counter, stored):
        offset = counter * column_block
        block_pos = lax.dynamic_slice_in_dim(gathered_pos, offset, column_block, 1)
        block_area = lax.dynamic_slice_in_dim(gathered_area, offset, column_block, 0)
        tile = kernel_tile(near, block_pos, block_area, scale)
        return lax.dynamic_update_slice_in_dim(stored, tile, offset, 1)

    self_rows = lax.fori_loop(
        0, total_cols // column_block, build_step, jnp.zeros((rows_here, total_cols), jnp.float32)
    )

    def apply_self(field):
        product = lax.dot_general(
            lax.all_gather(field[None], "row", axis=2, tiled=True)[0],
            self_rows,
            (((1,), (1,)), ((), ())),
            precision=lax.Precision.HIGHEST,
            preferred_element_type=jnp.float32,
        )
        return diagonal[None, :] * field + product

    currents = jnp.zeros((width, rows_here), jnp.float32)
    residual = excitation[0]
    for outer_step in range(OUTER):
        if outer_step > 0:
            all_currents = lax.all_gather(currents[None], "sub", axis=0, tiled=True)
            mine = jnp.arange(subdomains, dtype=jnp.int32) == lax.axis_index("sub")
            my_adjacency = jnp.sum(jnp.where(mine[:, None], adjacency, 0), axis=0)
            my_lists = jnp.sum(jnp.where(mine[:, None, None], block_list, 0), axis=0)
            my_counts = jnp.sum(jnp.where(mine[:, None], block_count, 0), axis=0)
            first_block = lax.axis_index("row") * local_blocks
            global_ids = first_block + jnp.arange(local_blocks, dtype=jnp.int32)
            total = jnp.zeros((width, local_blocks, BLK), jnp.float32)
            for slot in range(adjacency.shape[1]):
                chosen = jnp.arange(subdomains, dtype=jnp.int32) == my_adjacency[slot]
                src_pos = pick_source(other_pos, chosen)
                src_area = pick_source(other_area, chosen)
                src_cur = pick_source(all_currents, chosen)
                tiles = kernel_tile(
                    near.reshape(3, local_blocks, BLK),
                    src_pos.reshape(3, local_blocks, BLK),
                    src_area.reshape(local_blocks, BLK),
                    COUPLE / math.sqrt(BLK),
                )
                coupling_product = jnp.einsum(
                    "bpq,ebq->ebp",
                    tiles,
                    src_cur.reshape(width, local_blocks, BLK),
                    precision=lax.Precision.HIGHEST,
                )
                listed = (my_lists[slot][:, None] == global_ids[None, :]) & (
                    jnp.arange(my_lists.shape[1], dtype=jnp.int32)[:, None] < my_counts[slot]
                )
                weight = jnp.sum(listed.astype(jnp.float32), axis=0)
                total = total + coupling_product * weight[None, :, None]
            coupled = total.reshape(width, rows_here)
            residual = residual - coupled
        image = apply_self(residual)
        second = apply_self(image)
        cross, square, res_second, img_second, sec_second = lax.psum(
            (
                jnp.sum(residual * image, axis=1),
                jnp.sum(image * image, axis=1),
                jnp.sum(residual * second, axis=1),
                jnp.sum(image * second, axis=1),
                jnp.sum(second * second, axis=1),
            ),
            "row",
        )
        first_alpha = cross / (square + EPS)
        currents = currents + first_alpha[:, None] * residual
        residual = residual - first_alpha[:, None] * image
        image = image - first_alpha[:, None] * second
        cross_next = (
            cross
            - first_alpha * res_second
            - first_alpha * square
            + first_alpha * first_alpha * img_second
        )
        square_next = (
            square - 2.0 * first_alpha * img_second + first_alpha * first_alpha * sec_second
        )
        next_alpha = cross_next / (square_next + EPS)
        currents = currents + next_alpha[:, None] * residual
        residual = residual - next_alpha[:, None] * image
    return (currents[None], residual[None])


def on_device(sizes, *arrays):
    excitation, adjacency = arrays[3], arrays[4]
    count = excitation.shape[2]
    square = sizes["row"] == sizes["sub"] == adjacency.shape[0] == 4
    if square and excitation.shape[1] == 8 and count % (2 * TILE) == 0:
        return on_plane(*arrays)
    return on_rows(*arrays)


def solution(mesh):
    in_specs = (
        P(("body", "sub"), None, "row"),
        P(("body", "sub"), "row"),
        P(("body", "sub"), "row"),
        P(("body", "sub"), None, "row"),
        P("body", None),
        P("body", None, None),
        P("body", None),
    )
    out_specs = (P(("body", "sub"), None, "row"), P(("body", "sub"), None, "row"))
    sizes = {name: mesh.shape[name] for name in ("row", "sub")}
    return jax.shard_map(
        functools.partial(on_device, sizes),
        mesh=mesh,
        in_specs=in_specs,
        out_specs=out_specs,
        check_vma=False,
    )
```

```python
import functools
import math

import jax
import jax.numpy as jnp
from jax import lax
from jax.experimental import pallas as pl
from jax.experimental.pallas import tpu as pltpu
from jax.sharding import PartitionSpec as P

BLK = 32
OUTER = 2

KAPPA = 40.0
COUPLE = 1.0
EPS = 1e-06
column_block = 2048

F32 = jnp.float32
BF16 = jnp.bfloat16
TILE = 256
CHUNK = 32
FEATURES = 96
WAVE = KAPPA / (2.0 * math.pi)
ROUNDER = 12582912.0
HALF_COSINE = (
    0.9999982896004456,
    -4.934458936893249,
    4.048771939331772,
    -1.2478000348360374,
)
LIFT = 65536.0
FP8 = jnp.float8_e4m3fn
FP8_PEAK = 224.0


def to_grid(x, step):
    shift = ROUNDER * step
    return (x + shift) - shift


def cos_and_one(turns, amplitude):
    u = turns - jnp.round(turns)
    s = u * u
    factor = math.sqrt(2.0 * amplitude)
    value = HALF_COSINE[-1] * factor
    for coefficient in HALF_COSINE[-2::-1]:
        value = value * s + coefficient * factor
    return value * value


def green(squared_turns):
    y = jnp.maximum(squared_turns, 1e-12)
    turns = y * lax.rsqrt(y)
    amplitude = WAVE * LIFT
    return (cos_and_one(turns, amplitude) - amplitude) / (turns + WAVE)


def features(points):
    row = lax.broadcasted_iota(jnp.int32, points.shape, 0)
    centred = jnp.where(row < 3, (points - 0.5) * WAVE, 0.0)
    high = to_grid(centred, 2.0**-6)
    rest = centred - high
    mid = to_grid(rest, 2.0**-14)
    low = rest - mid
    coarse = jnp.sum(high * high, axis=0, keepdims=True)
    fine = jnp.sum(2.0 * high * rest + rest * rest, axis=0, keepdims=True)
    a = to_grid(coarse, 0.25)
    b = to_grid(coarse - a, 2.0**-10)
    c = coarse - a - b
    d = fine.astype(BF16).astype(F32)
    e = (fine - d).astype(BF16).astype(F32)
    f = fine - d - e
    norm = jnp.zeros_like(centred)
    for k, piece in enumerate((a, b, c, d, e, f)):
        norm = jnp.where(row == k, piece, norm)
    one = jnp.where(row < 6, 1.0, 0.0)
    zero = jnp.zeros_like(centred)
    left = (high, norm, one, high, mid, high, low, mid, mid, low, low, zero)
    right = (high, one, norm, mid, high, low, high, mid, low, mid, low, zero)
    right = tuple(-2.0 * x if k not in (1, 2) else x for k, x in enumerate(right))
    return left, right


def two_pieces(x):
    high = x.astype(BF16).astype(F32)
    return jnp.concatenate([high, x - high], axis=0).astype(BF16)


def fp8_piece(x):
    peak = jnp.maximum(jnp.max(jnp.abs(x), axis=1, keepdims=True), 1e-30)
    return (x * (FP8_PEAK / peak)).astype(FP8), peak * (1.0 / FP8_PEAK)


def nn(left, right):
    return lax.dot_general(left, right, (((1,), (0,)), ((), ())), preferred_element_type=F32)


def nt(left, right):
    return lax.dot_general(left, right, (((1,), (1,)), ((), ())), preferred_element_type=F32)


def prep_kernel(scale, doubled, pack_ref, left_ref, right_ref, field_ref, small_ref, undo_ref):
    pack = pack_ref[...]
    count = pack.shape[1]
    left, right = features(pack[:8])
    right = jnp.concatenate(right, axis=0).astype(BF16)
    weighted = pack[8:] * (pack[3:4] * (scale / LIFT))
    field = two_pieces(weighted)
    small, undo = fp8_piece(weighted)
    undo_ref[...] = jnp.broadcast_to(undo, undo_ref.shape)
    if doubled:
        for k in range(2):
            right_ref[:, k * count : (k + 1) * count] = right
            field_ref[:, k * count : (k + 1) * count] = field
            small_ref[:, k * count : (k + 1) * count] = small
        left = jnp.concatenate(left + (jnp.zeros((128 - FEATURES, count), F32),), axis=0)
        for k in range(count // TILE):
            left_ref[k * TILE : (k + 1) * TILE, :] = left[:, k * TILE : (k + 1) * TILE].T.astype(BF16)
    else:
        half = count // 2
        for k in range(count // TILE):
            to = (k % 2) * half + (k // 2) * TILE
            right_ref[:, to : to + TILE] = right[:, k * TILE : (k + 1) * TILE]
            field_ref[:, to : to + TILE] = field[:, k * TILE : (k + 1) * TILE]
            small_ref[:, to : to + TILE] = small[:, k * TILE : (k + 1) * TILE]


def fill_tile(source, at, target_high, target_low, to):
    for c in range(TILE // CHUNK):
        rows = slice(c * CHUNK, (c + 1) * CHUNK)
        g = green(source[rows, at : at + TILE])
        high = g.astype(BF16)
        target_high[rows, to : to + TILE] = high
        target_low[rows, to : to + TILE] = (g - high.astype(F32)).astype(FP8)


def fold_pieces(x):
    return x[:8] + x[8:]


def build_own_kernel(
    left_ref, right_ref, field_ref, small_ref, undo_ref, high_ref, low_ref, acc_ref, dist
):
    i = pl.program_id(0)
    width = high_ref.shape[1]
    tiles = width // TILE
    here = pl.multiple_of(i * TILE, TILE)

    @pl.when(i == 0)
    def _():
        acc_ref[...] = jnp.zeros_like(acc_ref)

    dist[...] = nn(
        left_ref[pl.ds(here, TILE), :FEATURES], right_ref[:, pl.ds(here, width)]
    )
    mine = field_ref[:, pl.ds(here, TILE)]
    mine_small = small_ref[:, pl.ds(here, TILE)]
    undo = undo_ref[:, :1]
    total = jnp.zeros((8, TILE), F32)
    for k in range(tiles):
        fill_tile(dist, k * TILE, high_ref, low_ref, k * TILE)
        there = pl.ds(pl.multiple_of(here + k * TILE, TILE), TILE)
        high = high_ref[:, k * TILE : (k + 1) * TILE]
        low = low_ref[:, k * TILE : (k + 1) * TILE]
        total += fold_pieces(nt(field_ref[:, there], high)) + nt(small_ref[:, there], low) * undo
        if 0 < k < tiles - 1:
            acc_ref[:, there] += fold_pieces(nn(mine, high)) + nn(mine_small, low) * undo
    acc_ref[:, pl.ds(here, TILE)] += total


def write_partial(part_ref, acc_own, acc_oth):
    count = acc_own.shape[1] // 2
    half = count // 2
    part_ref[:, :count] = acc_own[:, :count] + acc_own[:, count:]
    for b in range(3):
        for k in range(count // TILE):
            at = b * count + (k % 2) * half + (k // 2) * TILE
            to = (b + 1) * count + k * TILE
            part_ref[:, to : to + TILE] = acc_oth[:, at : at + TILE]


def build_oth_kernel(
    parity_ref, left_ref, right_ref, own_ref, own_small_ref, own_undo_ref,
    field_ref, small_ref, undo_ref, acc_in_ref,
    high_ref, low_ref, part_ref, dist, acc_own, acc_oth,
):
    i = pl.program_id(0)
    count = left_ref.shape[0]
    half = count // 2
    tiles = half // TILE
    here = pl.multiple_of(i * TILE, TILE)

    @pl.when(i == 0)
    def _():
        acc_own[...] = acc_in_ref[...]
        acc_oth[...] = jnp.zeros_like(acc_oth)

    offsets = [
        pl.multiple_of(b * count + ((i + parity_ref[b]) & 1) * half, TILE) for b in range(3)
    ]
    left = left_ref[pl.ds(here, TILE), :FEATURES]
    mine = own_ref[:, pl.ds(here, TILE)]
    mine_small = own_small_ref[:, pl.ds(here, TILE)]
    mine_undo = own_undo_ref[:, :1]
    total = jnp.zeros((8, TILE), F32)
    dist[0] = nn(left, right_ref[:, pl.ds(offsets[0], half)])
    for b in range(3):
        if b < 2:
            dist[(b + 1) % 2] = nn(left, right_ref[:, pl.ds(offsets[b + 1], half)])
        undo = undo_ref[:, b * 128 : b * 128 + 1]
        for k in range(tiles):
            to = b * half + k * TILE
            fill_tile(dist.at[b % 2], k * TILE, high_ref, low_ref, to)
            there = pl.ds(pl.multiple_of(offsets[b] + k * TILE, TILE), TILE)
            high = high_ref[:, to : to + TILE]
            low = low_ref[:, to : to + TILE]
            total += fold_pieces(nt(field_ref[:, there], high)) + nt(small_ref[:, there], low) * undo
            acc_oth[:, there] += fold_pieces(nn(mine, high)) + nn(mine_small, low) * mine_undo
    acc_own[:, pl.ds(here, TILE)] += total

    @pl.when(i == pl.num_programs(0) - 1)
    def _():
        write_partial(part_ref, acc_own, acc_oth)


def mr_step(even_ref, odd_ref, pack_ref, res_ref, cur_ref, new_res_ref, new_cur_ref):
    count = even_ref.shape[1] // 2
    image = []
    numerator = 0.0
    denominator = 0.0
    for b in range(4):
        source = odd_ref if b % 2 else even_ref
        product = source[:, (b // 2) * count : (b // 2 + 1) * count]
        cols = slice(b * count, (b + 1) * count)
        res = res_ref[:, cols]
        img = pack_ref[4:5, cols] * res + product
        new_res_ref[:, cols] = img
        numerator = numerator + jnp.sum(res * img, axis=1, keepdims=True)
        denominator = denominator + jnp.sum(img * img, axis=1, keepdims=True)
    alpha = numerator / (denominator + EPS)
    for b in range(4):
        cols = slice(b * count, (b + 1) * count)
        res = res_ref[:, cols]
        if cur_ref is None:
            new_cur_ref[:, cols] = alpha * res
        else:
            new_cur_ref[:, cols] = cur_ref[:, cols] + alpha * res
        new_res_ref[:, cols] = res - alpha * new_res_ref[:, cols]


def step_kernel(even_ref, odd_ref, pack_ref, res_ref, cur_ref, new_res_ref, new_cur_ref):
    mr_step(even_ref, odd_ref, pack_ref, res_ref, cur_ref, new_res_ref, new_cur_ref)


def apply_kernel(scale, first, couple, *refs):
    refs = list(refs)
    parity_ref = refs.pop(0)
    even_ref, odd_ref, pack_ref, res_ref = refs[:4]
    refs = refs[4:]
    cur_ref = None if first or couple else refs.pop(0)
    own_high, own_low, oth_high, oth_low = refs[:4]
    refs = refs[4:]
    new_res_ref = refs.pop(0)
    new_cur_ref = None if couple else refs.pop(0)
    part_ref, own_field, oth_field, own_small, oth_small, undos, acc_own, acc_oth = refs

    i = pl.program_id(0)
    count = even_ref.shape[1] // 2
    half = count // 2
    here = pl.multiple_of(i * TILE, TILE)

    @pl.when(i == 0)
    def _():
        acc_own[...] = jnp.zeros_like(acc_own)
        acc_oth[...] = jnp.zeros_like(acc_oth)
        if couple:
            for b in range(4):
                source = odd_ref if b % 2 else even_ref
                cols = slice(b * count, (b + 1) * count)
                new_res_ref[:, cols] = (
                    res_ref[:, cols] - source[:, (b // 2) * count : (b // 2 + 1) * count]
                )
        else:
            mr_step(even_ref, odd_ref, pack_ref, res_ref, cur_ref, new_res_ref, new_cur_ref)
        for b in range(4):
            cols = slice(b * count, (b + 1) * count)
            weighted = new_res_ref[:, cols] * (pack_ref[3:4, cols] * (scale / LIFT))
            field = two_pieces(weighted)
            small, undo = fp8_piece(weighted)
            undos[:, b * 128 : (b + 1) * 128] = jnp.broadcast_to(undo, (8, 128))
            if b == 0:
                for k in range(2):
                    own_field[:, k * count : (k + 1) * count] = field
                    own_small[:, k * count : (k + 1) * count] = small
                continue
            for k in range(count // TILE):
                to = (b - 1) * count + (k % 2) * half + (k // 2) * TILE
                oth_field[:, to : to + TILE] = field[:, k * TILE : (k + 1) * TILE]
                oth_small[:, to : to + TILE] = small[:, k * TILE : (k + 1) * TILE]

    width = own_high.shape[1]
    mine = own_field[:, pl.ds(here, TILE)]
    mine_small = own_small[:, pl.ds(here, TILE)]
    undo = undos[:, :1]
    span = pl.ds(here, width)
    inner = pl.ds(pl.multiple_of(here + TILE, TILE), width - 2 * TILE)
    total = fold_pieces(nt(own_field[:, span], own_high[...]))
    total += nt(own_small[:, span], own_low[...]) * undo
    acc_own[:, inner] += (
        fold_pieces(nn(mine, own_high[:, TILE : width - TILE]))
        + nn(mine_small, own_low[:, TILE : width - TILE]) * undo
    )
    for b in range(3):
        there = pl.ds(
            pl.multiple_of(b * count + ((i + parity_ref[b]) & 1) * half, TILE), half
        )
        high = oth_high[:, b * half : (b + 1) * half]
        low = oth_low[:, b * half : (b + 1) * half]
        total += fold_pieces(nt(oth_field[:, there], high))
        total += nt(oth_small[:, there], low) * undos[:, (b + 1) * 128 : (b + 1) * 128 + 1]
        acc_oth[:, there] += fold_pieces(nn(mine, high)) + nn(mine_small, low) * undo
    acc_own[:, pl.ds(here, TILE)] += total

    @pl.when(i == pl.num_programs(0) - 1)
    def _():
        write_partial(part_ref, acc_own, acc_oth)


def couple_kernel(source_ref, list_ref, count_ref, first_ref, near_ref, far_ref, cur_ref, out_ref):
    count = near_ref.shape[1]
    lane = lax.broadcasted_iota(jnp.int32, (1, count), 1)
    ident = first_ref[0] + lane // BLK
    row = lax.broadcasted_iota(jnp.int32, (128, 128), 0) // BLK
    col = lax.broadcasted_iota(jnp.int32, (128, 128), 1) // BLK
    same = row == col
    total = None
    weights = []
    for slot in range(count_ref.shape[0]):
        hits = jnp.zeros((1, count), F32)
        for k in range(list_ref.shape[1]):
            hit = (ident == list_ref[slot, k]) & (k < count_ref[slot])
            hits = hits + jnp.where(hit, 1.0, 0.0)
        weights.append(hits)
    for g in range(count // 128):
        cols = slice(g * 128, (g + 1) * 128)
        near = near_ref[:8, cols].T
        total = jnp.zeros((8, 128), F32)
        for slot in range(count_ref.shape[0]):
            far = far_ref[source_ref[slot], :, cols]
            squared = jnp.zeros((128, 128), F32)
            for x in range(3):
                gap = near[:, x : x + 1] - far[x : x + 1, :]
                squared = squared + gap * gap
            safe = jnp.maximum(squared, 1e-30)
            radius = safe * lax.rsqrt(safe)
            tile = (cos_and_one(radius * WAVE, 1.0) - 1.0) / (1.0 + radius)
            tile = jnp.where(same, tile, 0.0)
            field = cur_ref[source_ref[slot], :, cols] * (far[3:4, :] * (COUPLE / math.sqrt(BLK)))
            high = tile.astype(BF16)
            low = (tile - high.astype(F32)).astype(BF16)
            pieces = two_pieces(field)
            product = nt(pieces, high) + nt(pieces, low)
            total = total + fold_pieces(product) * weights[slot][:, cols]
        out_ref[:, cols] = total


def whole(shape):
    return pl.BlockSpec(shape, lambda i, *_: (0,) * len(shape))


SMEM = pl.BlockSpec(memory_space=pltpu.SMEM)
VMEM_LIMIT = 48 * 1024 * 1024


def params(**kw):
    return pltpu.CompilerParams(vmem_limit_bytes=VMEM_LIMIT, **kw)


def on_plane(positions, panel_area, self_term, excitation, adjacency, block_list, block_count):
    count = excitation.shape[2]
    subs = adjacency.shape[0]
    ranks = subs
    unknowns = count * ranks
    scale = 1.0 / math.sqrt(unknowns)
    tiles = count // TILE
    half = count // 2
    own_width = (tiles // 2 + 1) * TILE
    plane = lax.axis_index("row")
    place = lax.axis_index("sub")

    swap = [(z * subs + s, s * subs + z) for z in range(ranks) for s in range(subs)]

    def over(bit):
        return [(s, s ^ bit) for s in range(subs)]

    def send(x, bit):
        return lax.ppermute(x, "sub", over(bit))

    pack = jnp.concatenate(
        [
            positions[0],
            panel_area,
            self_term,
            jnp.zeros((3, count), F32),
            excitation[0],
        ],
        axis=0,
    )
    pack = lax.ppermute(pack, ("row", "sub"), swap)

    f32 = lambda *s: jax.ShapeDtypeStruct(s, F32)
    b16 = lambda *s: jax.ShapeDtypeStruct(s, BF16)
    fp8 = lambda *s: jax.ShapeDtypeStruct(s, FP8)

    left, right_own, field_own, small_own, undo_own = pl.pallas_call(
        functools.partial(prep_kernel, scale, True),
        out_shape=(
            b16(count, 128),
            b16(FEATURES, 2 * count),
            b16(16, 2 * count),
            fp8(8, 2 * count),
            f32(8, 128),
        ),
        compiler_params=params(),
        name="prep_own",
    )(pack)

    pack2 = send(pack, 2)
    packs = jnp.stack([pack, pack2])
    packs_odd = send(packs, 1)
    full = jnp.concatenate([pack, packs_odd[0], pack2, packs_odd[1]], axis=1)

    own_high, own_low, acc = pl.pallas_call(
        build_own_kernel,
        grid=(tiles,),
        in_specs=[
            whole((count, 128)),
            whole((FEATURES, 2 * count)),
            whole((16, 2 * count)),
            whole((8, 2 * count)),
            whole((8, 128)),
        ],
        out_specs=(
            pl.BlockSpec((TILE, own_width), lambda i: (i, 0)),
            pl.BlockSpec((TILE, own_width), lambda i: (i, 0)),
            whole((8, 2 * count)),
        ),
        out_shape=(b16(count, own_width), fp8(count, own_width), f32(8, 2 * count)),
        scratch_shapes=[pltpu.VMEM((TILE, own_width), F32)],
        compiler_params=params(),
        cost_estimate=pl.CostEstimate(
            flops=60 * count * own_width, bytes_accessed=4 * count * own_width, transcendentals=0
        ),
        name="build_own",
    )(left, right_own, field_own, small_own, undo_own)

    others = []
    for b in range(1, 4):
        others.append(
            pl.pallas_call(
                lambda p, *outs: prep_kernel(scale, False, p, None, *outs),
                out_shape=(b16(FEATURES, count), b16(16, count), fp8(8, count), f32(8, 128)),
                compiler_params=params(),
                name="prep_oth",
            )(full[:, b * count : (b + 1) * count])
        )
    right_oth, field_oth, small_oth, undo_oth = (
        jnp.concatenate(parts, axis=1) for parts in zip(*others)
    )

    parity = jnp.stack([(place > (place ^ b)).astype(jnp.int32) for b in range(1, 4)])

    oth_high, oth_low, part = pl.pallas_call(
        build_oth_kernel,
        grid_spec=pltpu.PrefetchScalarGridSpec(
            num_scalar_prefetch=1,
            grid=(tiles,),
            in_specs=[
                whole((count, 128)),
                whole((FEATURES, 3 * count)),
                whole((16, 2 * count)),
                whole((8, 2 * count)),
                whole((8, 128)),
                whole((16, 3 * count)),
                whole((8, 3 * count)),
                whole((8, 3 * 128)),
                whole((8, 2 * count)),
            ],
            out_specs=(
                pl.BlockSpec((TILE, 3 * half), lambda i, *_: (i, 0)),
                pl.BlockSpec((TILE, 3 * half), lambda i, *_: (i, 0)),
                whole((8, 4 * count)),
            ),
            scratch_shapes=[
                pltpu.VMEM((2, TILE, half), F32),
                pltpu.VMEM((8, 2 * count), F32),
                pltpu.VMEM((8, 3 * count), F32),
            ],
        ),
        out_shape=(b16(count, 3 * half), fp8(count, 3 * half), f32(8, 4 * count)),
        compiler_params=params(),
        name="build_oth",
    )(
        parity, left, right_oth, field_own, small_own, undo_own,
        field_oth, small_oth, undo_oth, acc,
    )

    def pair(x, a, b):
        return jnp.concatenate(
            [x[:, a * count : (a + 1) * count], x[:, b * count : (b + 1) * count]], axis=1
        )

    def reduce_all(part):
        got = send(pair(part, 1, 3), 1)
        chip = pair(part, 0, 2) + got
        got = send(chip, 2)
        even = chip + pair(got, 1, 0)
        odd = send(even, 1)
        return even, odd

    def apply(even, odd, res, cur, couple):
        first = cur is None and not couple
        operands = [even, odd, full, res]
        specs = [
            whole((8, 2 * count)),
            whole((8, 2 * count)),
            whole((16, 4 * count)),
            whole((8, 4 * count)),
        ]
        if not first and not couple:
            operands.append(cur)
            specs.append(whole((8, 4 * count)))
        own_spec = pl.BlockSpec((TILE, own_width), lambda i, *_: (i, 0))
        oth_spec = pl.BlockSpec((TILE, 3 * half), lambda i, *_: (i, 0))
        operands += [own_high, own_low, oth_high, oth_low]
        specs += [own_spec, own_spec, oth_spec, oth_spec]
        outs = 2 if couple else 3
        return pl.pallas_call(
            functools.partial(apply_kernel, scale, first, couple),
            grid_spec=pltpu.PrefetchScalarGridSpec(
                num_scalar_prefetch=1,
                grid=(tiles,),
                in_specs=specs,
                out_specs=[whole((8, 4 * count))] * outs,
                scratch_shapes=[
                    pltpu.VMEM((16, 2 * count), BF16),
                    pltpu.VMEM((16, 3 * count), BF16),
                    pltpu.VMEM((8, 2 * count), FP8),
                    pltpu.VMEM((8, 3 * count), FP8),
                    pltpu.VMEM((8, 4 * 128), F32),
                    pltpu.VMEM((8, 2 * count), F32),
                    pltpu.VMEM((8, 3 * count), F32),
                ],
            ),
            out_shape=[f32(8, 4 * count)] * outs,
            compiler_params=params(),
            name="apply",
        )(parity, *operands)

    even, odd = reduce_all(part)
    res, cur, part = apply(even, odd, full[8:], None, False)
    even, odd = reduce_all(part)
    res, cur = pl.pallas_call(
        step_kernel,
        out_shape=[f32(8, 4 * count)] * 2,
        compiler_params=params(),
        name="step",
    )(even, odd, full, res, cur)

    def from_planes(x):
        return jnp.stack(
            [
                lax.ppermute(x, "row", [(z, (z + k) % ranks) for z in range(ranks)])
                for k in range(1, ranks)
            ]
        )

    far = from_planes(pack[:8])
    far_cur = from_planes(cur[:, :count])
    mine = jnp.arange(subs, dtype=jnp.int32) == plane
    neighbours = jnp.sum(jnp.where(mine[:, None], adjacency, 0), axis=0)
    lists = jnp.sum(jnp.where(mine[:, None, None], block_list, 0), axis=0)
    counts = jnp.sum(jnp.where(mine[:, None], block_count, 0), axis=0)
    source = (plane - neighbours + subs) % subs - 1
    first_block = (place * (count // BLK)).astype(jnp.int32).reshape(1)
    coupled = pl.pallas_call(
        couple_kernel,
        in_specs=[SMEM] * 4 + [pl.BlockSpec(memory_space=pltpu.VMEM)] * 3,
        out_shape=f32(8, count),
        compiler_params=params(),
        name="couple",
    )(source, lists, counts, first_block, pack, far, far_cur)
    even = jnp.concatenate([coupled, send(coupled, 2)], axis=1)
    odd = send(even, 1)

    res, part = apply(even, odd, res, None, True)
    even, odd = reduce_all(part)
    res, cur, part = apply(even, odd, res, cur, False)
    even, odd = reduce_all(part)
    res, cur = pl.pallas_call(
        step_kernel,
        out_shape=[f32(8, 4 * count)] * 2,
        compiler_params=params(),
        name="step",
    )(even, odd, full, res, cur)
    out = jnp.concatenate([cur[:, :count], res[:, :count]], axis=0)
    out = lax.ppermute(out, ("row", "sub"), swap)
    return out[None, :8], out[None, 8:]


def kernel_tile(near, far, area, scale):
    squared = jnp.zeros(near.shape[1:] + far.shape[-1:], jnp.float32)
    for coord in range(3):
        spacing = near[coord][..., :, None] - far[coord][..., None, :]
        squared = squared + spacing * spacing
    radius = jnp.sqrt(squared)
    return jnp.cos(KAPPA * radius) / (1.0 + radius) * (area * scale)[..., None, :]


def pick_source(table, chosen):
    shaped = chosen.reshape(chosen.shape + (1,) * (table.ndim - 1))
    return jnp.sum(jnp.where(shaped, table, jnp.zeros_like(table)), axis=0)


def on_rows(positions, panel_area, self_term, excitation, adjacency, block_list, block_count):
    width = excitation.shape[1]
    rows_here = excitation.shape[2]
    near = positions[0]
    diagonal = self_term[0]
    gathered_pos, gathered_area = (
        lax.all_gather(positions[0], "row", axis=1, tiled=True),
        lax.all_gather(panel_area[0], "row", axis=0, tiled=True),
    )
    other_pos, other_area = (
        lax.all_gather(positions, "sub", axis=0, tiled=True),
        lax.all_gather(panel_area, "sub", axis=0, tiled=True),
    )
    total_cols = gathered_pos.shape[1]
    scale = 1.0 / math.sqrt(total_cols)
    subdomains = adjacency.shape[0]
    local_blocks = rows_here // BLK

    def build_step(counter, stored):
        offset = counter * column_block
        block_pos = lax.dynamic_slice_in_dim(gathered_pos, offset, column_block, 1)
        block_area = lax.dynamic_slice_in_dim(gathered_area, offset, column_block, 0)
        tile = kernel_tile(near, block_pos, block_area, scale)
        return lax.dynamic_update_slice_in_dim(stored, tile, offset, 1)

    self_rows = lax.fori_loop(
        0, total_cols // column_block, build_step, jnp.zeros((rows_here, total_cols), jnp.float32)
    )

    def apply_self(field):
        product = lax.dot_general(
            lax.all_gather(field[None], "row", axis=2, tiled=True)[0],
            self_rows,
            (((1,), (1,)), ((), ())),
            precision=lax.Precision.HIGHEST,
            preferred_element_type=jnp.float32,
        )
        return diagonal[None, :] * field + product

    currents = jnp.zeros((width, rows_here), jnp.float32)
    residual = excitation[0]
    for outer_step in range(OUTER):
        if outer_step > 0:
            all_currents = lax.all_gather(currents[None], "sub", axis=0, tiled=True)
            mine = jnp.arange(subdomains, dtype=jnp.int32) == lax.axis_index("sub")
            my_adjacency = jnp.sum(jnp.where(mine[:, None], adjacency, 0), axis=0)
            my_lists = jnp.sum(jnp.where(mine[:, None, None], block_list, 0), axis=0)
            my_counts = jnp.sum(jnp.where(mine[:, None], block_count, 0), axis=0)
            first_block = lax.axis_index("row") * local_blocks
            global_ids = first_block + jnp.arange(local_blocks, dtype=jnp.int32)
            total = jnp.zeros((width, local_blocks, BLK), jnp.float32)
            for slot in range(adjacency.shape[1]):
                chosen = jnp.arange(subdomains, dtype=jnp.int32) == my_adjacency[slot]
                src_pos = pick_source(other_pos, chosen)
                src_area = pick_source(other_area, chosen)
                src_cur = pick_source(all_currents, chosen)
                tiles = kernel_tile(
                    near.reshape(3, local_blocks, BLK),
                    src_pos.reshape(3, local_blocks, BLK),
                    src_area.reshape(local_blocks, BLK),
                    COUPLE / math.sqrt(BLK),
                )
                coupling_product = jnp.einsum(
                    "bpq,ebq->ebp",
                    tiles,
                    src_cur.reshape(width, local_blocks, BLK),
                    precision=lax.Precision.HIGHEST,
                )
                listed = (my_lists[slot][:, None] == global_ids[None, :]) & (
                    jnp.arange(my_lists.shape[1], dtype=jnp.int32)[:, None] < my_counts[slot]
                )
                weight = jnp.sum(listed.astype(jnp.float32), axis=0)
                total = total + coupling_product * weight[None, :, None]
            coupled = total.reshape(width, rows_here)
            residual = residual - coupled
        image = apply_self(residual)
        second = apply_self(image)
        cross, square, res_second, img_second, sec_second = lax.psum(
            (
                jnp.sum(residual * image, axis=1),
                jnp.sum(image * image, axis=1),
                jnp.sum(residual * second, axis=1),
                jnp.sum(image * second, axis=1),
                jnp.sum(second * second, axis=1),
            ),
            "row",
        )
        first_alpha = cross / (square + EPS)
        currents = currents + first_alpha[:, None] * residual
        residual = residual - first_alpha[:, None] * image
        image = image - first_alpha[:, None] * second
        cross_next = (
            cross
            - first_alpha * res_second
            - first_alpha * square
            + first_alpha * first_alpha * img_second
        )
        square_next = (
            square - 2.0 * first_alpha * img_second + first_alpha * first_alpha * sec_second
        )
        next_alpha = cross_next / (square_next + EPS)
        currents = currents + next_alpha[:, None] * residual
        residual = residual - next_alpha[:, None] * image
    return (currents[None], residual[None])


def on_device(sizes, *arrays):
    excitation, adjacency = arrays[3], arrays[4]
    count = excitation.shape[2]
    square = sizes["row"] == sizes["sub"] == adjacency.shape[0] == 4
    if square and excitation.shape[1] == 8 and count % (2 * TILE) == 0:
        return on_plane(*arrays)
    return on_rows(*arrays)


def solution(mesh):
    in_specs = (
        P(("body", "sub"), None, "row"),
        P(("body", "sub"), "row"),
        P(("body", "sub"), "row"),
        P(("body", "sub"), None, "row"),
        P("body", None),
        P("body", None, None),
        P("body", None),
    )
    out_specs = (P(("body", "sub"), None, "row"), P(("body", "sub"), None, "row"))
    sizes = {name: mesh.shape[name] for name in ("row", "sub")}
    return jax.shard_map(
        functools.partial(on_device, sizes),
        mesh=mesh,
        in_specs=in_specs,
        out_specs=out_specs,
        check_vma=False,
    )
```

```python
import functools
import math

import jax
import jax.numpy as jnp
from jax import lax
from jax.experimental import pallas as pl
from jax.experimental.pallas import tpu as pltpu
from jax.sharding import PartitionSpec as P


BLK = 32
OUTER = 2

KAPPA = 40.0
COUPLE = 1.0
EPS = 1e-06
column_block = 2048

F32 = jnp.float32
BF16 = jnp.bfloat16
TILE = 256
CHUNK = 32
FEATURES = 96
WAVE = KAPPA / (2.0 * math.pi)
ROUNDER = 12582912.0
HALF_COSINE = (
    0.9999982896004456,
    -4.934458936893249,
    4.048771939331772,
    -1.2478000348360374,
)
LIFT = 65536.0
FP8 = jnp.float8_e4m3fn
FP8_PEAK = 224.0


def to_grid(x, step):
    shift = ROUNDER * step
    return (x + shift) - shift


def cos_and_one(turns, amplitude):
    u = turns - jnp.round(turns)
    s = u * u
    factor = math.sqrt(2.0 * amplitude)
    value = HALF_COSINE[-1] * factor
    for coefficient in HALF_COSINE[-2::-1]:
        value = value * s + coefficient * factor
    return value * value


def green(squared_turns):
    y = jnp.maximum(squared_turns, 1e-12)
    turns = y * lax.rsqrt(y)
    amplitude = WAVE * LIFT
    return (cos_and_one(turns, amplitude) - amplitude) / (turns + WAVE)


def features(points):
    row = lax.broadcasted_iota(jnp.int32, points.shape, 0)
    centred = jnp.where(row < 3, (points - 0.5) * WAVE, 0.0)
    high = to_grid(centred, 2.0**-6)
    rest = centred - high
    mid = to_grid(rest, 2.0**-14)
    low = rest - mid
    coarse = jnp.sum(high * high, axis=0, keepdims=True)
    fine = jnp.sum(2.0 * high * rest + rest * rest, axis=0, keepdims=True)
    a = to_grid(coarse, 0.25)
    b = to_grid(coarse - a, 2.0**-10)
    c = coarse - a - b
    d = fine.astype(BF16).astype(F32)
    e = (fine - d).astype(BF16).astype(F32)
    f = fine - d - e
    norm = jnp.zeros_like(centred)
    for k, piece in enumerate((a, b, c, d, e, f)):
        norm = jnp.where(row == k, piece, norm)
    one = jnp.where(row < 6, 1.0, 0.0)
    zero = jnp.zeros_like(centred)
    left = (high, norm, one, high, mid, high, low, mid, mid, low, low, zero)
    right = (high, one, norm, mid, high, low, high, mid, low, mid, low, zero)
    right = tuple(-2.0 * x if k not in (1, 2) else x for k, x in enumerate(right))
    return left, right


def two_pieces(x):
    high = x.astype(BF16).astype(F32)
    return jnp.concatenate([high, x - high], axis=0).astype(BF16)


def fp8_piece(x):
    peak = jnp.maximum(jnp.max(jnp.abs(x), axis=1, keepdims=True), 1e-30)
    return (x * (FP8_PEAK / peak)).astype(FP8), peak * (1.0 / FP8_PEAK)


def nn(left, right):
    return lax.dot_general(left, right, (((1,), (0,)), ((), ())), preferred_element_type=F32)


def nt(left, right):
    return lax.dot_general(left, right, (((1,), (1,)), ((), ())), preferred_element_type=F32)


def prep_kernel(scale, doubled, pack_ref, left_ref, right_ref, field_ref, small_ref, undo_ref):
    pack = pack_ref[...]
    count = pack.shape[1]
    left, right = features(pack[:8])
    right = jnp.concatenate(right, axis=0).astype(BF16)
    weighted = pack[8:] * (pack[3:4] * (scale / LIFT))
    field = two_pieces(weighted)
    small, undo = fp8_piece(weighted)
    undo_ref[...] = jnp.broadcast_to(undo, undo_ref.shape)
    if doubled:
        for k in range(2):
            right_ref[:, k * count : (k + 1) * count] = right
            field_ref[:, k * count : (k + 1) * count] = field
            small_ref[:, k * count : (k + 1) * count] = small
        left = jnp.concatenate(left + (jnp.zeros((128 - FEATURES, count), F32),), axis=0)
        for k in range(count // TILE):
            left_ref[k * TILE : (k + 1) * TILE, :] = left[:, k * TILE : (k + 1) * TILE].T.astype(BF16)
    else:
        half = count // 2
        for k in range(count // TILE):
            to = (k % 2) * half + (k // 2) * TILE
            right_ref[:, to : to + TILE] = right[:, k * TILE : (k + 1) * TILE]
            field_ref[:, to : to + TILE] = field[:, k * TILE : (k + 1) * TILE]
            small_ref[:, to : to + TILE] = small[:, k * TILE : (k + 1) * TILE]


def fill_tile(source, at, target_high, target_low, to):
    for c in range(TILE // CHUNK):
        rows = slice(c * CHUNK, (c + 1) * CHUNK)
        g = green(source[rows, at : at + TILE])
        high = g.astype(BF16)
        target_high[rows, to : to + TILE] = high
        target_low[rows, to : to + TILE] = (g - high.astype(F32)).astype(FP8)


def fold_pieces(x):
    return x[:8] + x[8:]


def build_own_kernel(
    left_ref, right_ref, field_ref, small_ref, undo_ref, high_ref, low_ref, acc_ref, dist
):
    i = pl.program_id(0)
    width = high_ref.shape[1]
    tiles = width // TILE
    here = pl.multiple_of(i * TILE, TILE)

    @pl.when(i == 0)
    def _():
        acc_ref[...] = jnp.zeros_like(acc_ref)

    dist[...] = nn(
        left_ref[pl.ds(here, TILE), :FEATURES], right_ref[:, pl.ds(here, width)]
    )
    mine = field_ref[:, pl.ds(here, TILE)]
    mine_small = small_ref[:, pl.ds(here, TILE)]
    undo = undo_ref[:, :1]
    total = jnp.zeros((8, TILE), F32)
    for k in range(tiles):
        fill_tile(dist, k * TILE, high_ref, low_ref, k * TILE)
        there = pl.ds(pl.multiple_of(here + k * TILE, TILE), TILE)
        high = high_ref[:, k * TILE : (k + 1) * TILE]
        low = low_ref[:, k * TILE : (k + 1) * TILE]
        total += fold_pieces(nt(field_ref[:, there], high)) + nt(small_ref[:, there], low) * undo
        if 0 < k < tiles - 1:
            acc_ref[:, there] += fold_pieces(nn(mine, high)) + nn(mine_small, low) * undo
    acc_ref[:, pl.ds(here, TILE)] += total


def write_partial(part_ref, acc_own, acc_oth):
    count = acc_own.shape[1] // 2
    half = count // 2
    part_ref[:, :count] = acc_own[:, :count] + acc_own[:, count:]
    for b in range(3):
        for k in range(count // TILE):
            at = b * count + (k % 2) * half + (k // 2) * TILE
            to = (b + 1) * count + k * TILE
            part_ref[:, to : to + TILE] = acc_oth[:, at : at + TILE]


def build_oth_kernel(
    parity_ref, left_ref, right_ref, own_ref, own_small_ref, own_undo_ref,
    field_ref, small_ref, undo_ref, acc_in_ref, far_ref,
    high_ref, low_ref, part_ref, dist, acc_own, acc_oth,
):
    i = pl.program_id(0)
    count = left_ref.shape[0]
    half = count // 2
    tiles = half // TILE
    here = pl.multiple_of(i * TILE, TILE)

    @pl.when(i == 0)
    def _():
        acc_own[...] = acc_in_ref[...]
        acc_oth[...] = jnp.zeros_like(acc_oth)

    offsets = [
        pl.multiple_of(b * count + ((i + parity_ref[b]) & 1) * half, TILE) for b in range(3)
    ]
    left = left_ref[pl.ds(here, TILE), :FEATURES]
    mine = own_ref[:, pl.ds(here, TILE)]
    mine_small = own_small_ref[:, pl.ds(here, TILE)]
    mine_undo = own_undo_ref[:, :1]
    total = jnp.zeros((8, TILE), F32)
    dist[0] = nn(left, right_ref[:, pl.ds(offsets[0], half)])
    for b in range(3):
        if b < 2:
            dist[(b + 1) % 2] = nn(left, right_ref[:, pl.ds(offsets[b + 1], half)])
        undo = undo_ref[:, b * 128 : b * 128 + 1]
        for k in range(tiles):
            to = b * half + k * TILE
            fill_tile(dist.at[b % 2], k * TILE, high_ref, low_ref, to)
            there = pl.ds(pl.multiple_of(offsets[b] + k * TILE, TILE), TILE)
            high = high_ref[:, to : to + TILE]
            low = low_ref[:, to : to + TILE]
            total += fold_pieces(nt(field_ref[:, there], high)) + nt(small_ref[:, there], low) * undo
            acc_oth[:, there] += fold_pieces(nn(mine, high)) + nn(mine_small, low) * mine_undo
    acc_own[:, pl.ds(here, TILE)] += total

    @pl.when(i == pl.num_programs(0) - 1)
    def _():
        write_partial(part_ref, acc_own, acc_oth)


def step_kernel(even_ref, odd_ref, pack_ref, res_ref, *refs):
    cur_ref = refs[0] if len(refs) == 4 else None
    new_res_ref, new_cur_ref, alpha_ref = refs[-3:]
    count = even_ref.shape[1] // 2
    numerator = 0.0
    denominator = 0.0
    for b in range(4):
        source = odd_ref if b % 2 else even_ref
        product = source[:, (b // 2) * count : (b // 2 + 1) * count]
        cols = slice(b * count, (b + 1) * count)
        res = res_ref[:, cols]
        img = pack_ref[4:5, cols] * res + product
        new_res_ref[:, cols] = img
        numerator = numerator + jnp.sum(res * img, axis=1, keepdims=True)
        denominator = denominator + jnp.sum(img * img, axis=1, keepdims=True)
    alpha = numerator / (denominator + EPS)
    alpha_ref[...] = jnp.broadcast_to(alpha, alpha_ref.shape)
    for b in range(4):
        cols = slice(b * count, (b + 1) * count)
        res = res_ref[:, cols]
        if cur_ref is None:
            new_cur_ref[:, cols] = alpha * res
        else:
            new_cur_ref[:, cols] = cur_ref[:, cols] + alpha * res
        new_res_ref[:, cols] = res - alpha * new_res_ref[:, cols]


def apply_kernel(
    scale, parity_ref, pack_ref, res_ref, own_high, own_low, oth_high, oth_low,
    part_ref, own_field, oth_field, own_small, oth_small, undos, acc_own, acc_oth,
):
    i = pl.program_id(0)
    count = res_ref.shape[1] // 4
    half = count // 2
    here = pl.multiple_of(i * TILE, TILE)

    @pl.when(i == 0)
    def _():
        acc_own[...] = jnp.zeros_like(acc_own)
        acc_oth[...] = jnp.zeros_like(acc_oth)
        for b in range(4):
            cols = slice(b * count, (b + 1) * count)
            weighted = res_ref[:, cols] * (pack_ref[3:4, cols] * (scale / LIFT))
            field = two_pieces(weighted)
            small, undo = fp8_piece(weighted)
            undos[:, b * 128 : (b + 1) * 128] = jnp.broadcast_to(undo, (8, 128))
            if b == 0:
                for k in range(2):
                    own_field[:, k * count : (k + 1) * count] = field
                    own_small[:, k * count : (k + 1) * count] = small
                continue
            for k in range(count // TILE):
                to = (b - 1) * count + (k % 2) * half + (k // 2) * TILE
                oth_field[:, to : to + TILE] = field[:, k * TILE : (k + 1) * TILE]
                oth_small[:, to : to + TILE] = small[:, k * TILE : (k + 1) * TILE]

    width = own_high.shape[1]
    mine = own_field[:, pl.ds(here, TILE)]
    mine_small = own_small[:, pl.ds(here, TILE)]
    undo = undos[:, :1]
    span = pl.ds(here, width)
    inner = pl.ds(pl.multiple_of(here + TILE, TILE), width - 2 * TILE)
    total = fold_pieces(nt(own_field[:, span], own_high[...]))
    total += nt(own_small[:, span], own_low[...]) * undo
    acc_own[:, inner] += (
        fold_pieces(nn(mine, own_high[:, TILE : width - TILE]))
        + nn(mine_small, own_low[:, TILE : width - TILE]) * undo
    )
    for b in range(3):
        there = pl.ds(
            pl.multiple_of(b * count + ((i + parity_ref[b]) & 1) * half, TILE), half
        )
        high = oth_high[:, b * half : (b + 1) * half]
        low = oth_low[:, b * half : (b + 1) * half]
        total += fold_pieces(nt(oth_field[:, there], high))
        total += nt(oth_small[:, there], low) * undos[:, (b + 1) * 128 : (b + 1) * 128 + 1]
        acc_oth[:, there] += fold_pieces(nn(mine, high)) + nn(mine_small, low) * undo
    acc_own[:, pl.ds(here, TILE)] += total

    @pl.when(i == pl.num_programs(0) - 1)
    def _():
        write_partial(part_ref, acc_own, acc_oth)


def interface_product(field, high, low):
    pieces = two_pieces(field)
    return fold_pieces(nt(pieces, high) + nt(pieces, low))


def couple_kernel(
    source_ref, list_ref, count_ref, first_ref, near_ref, far_ref,
    high_ref, low_ref, weight_ref, out_ref,
):
    count = near_ref.shape[1]
    slots = count_ref.shape[0]
    lane = lax.broadcasted_iota(jnp.int32, (1, count), 1)
    ident = first_ref[0] + lane // BLK
    row = lax.broadcasted_iota(jnp.int32, (128, 128), 0) // BLK
    col = lax.broadcasted_iota(jnp.int32, (128, 128), 1) // BLK
    same = row == col
    for slot in range(slots):
        hits = jnp.zeros((1, count), F32)
        for k in range(list_ref.shape[1]):
            hit = (ident == list_ref[slot, k]) & (k < count_ref[slot])
            hits = hits + jnp.where(hit, 1.0, 0.0)
        weight_ref[slot * 8 : slot * 8 + 8, :] = jnp.broadcast_to(hits, (8, count))
    for g in range(count // 128):
        cols = slice(g * 128, (g + 1) * 128)
        near = near_ref[:8, cols].T
        for slot in range(slots):
            far = far_ref[source_ref[slot], :, cols]
            squared = jnp.zeros((128, 128), F32)
            for x in range(3):
                gap = near[:, x : x + 1] - far[x : x + 1, :]
                squared = squared + gap * gap
            safe = jnp.maximum(squared, 1e-30)
            radius = safe * lax.rsqrt(safe)
            tile = (cos_and_one(radius * WAVE, 1.0) - 1.0) / (1.0 + radius)
            tile = jnp.where(same, tile * (far[3:4, :] * (COUPLE / math.sqrt(BLK))), 0.0)
            high = tile.astype(BF16)
            low = (tile - high.astype(F32)).astype(BF16)
            high_ref[slot, cols, :] = high
            low_ref[slot, cols, :] = low
            rows = slice(slot * 8, slot * 8 + 8)
            out_ref[rows, cols] = interface_product(far[8:], high, low) * weight_ref[rows, cols]


def couple_again_kernel(source_ref, high_ref, low_ref, weight_ref, far_ref, out_ref):
    for g in range(out_ref.shape[1] // 128):
        cols = slice(g * 128, (g + 1) * 128)
        for slot in range(source_ref.shape[0]):
            rows = slice(slot * 8, slot * 8 + 8)
            far = far_ref[source_ref[slot], :, cols]
            product = interface_product(far, high_ref[slot, cols, :], low_ref[slot, cols, :])
            out_ref[rows, cols] = product * weight_ref[rows, cols]


def combine_kernel(source_ref, alpha_ref, first_ref, second_ref, out_ref):
    total = 0.0
    for slot in range(source_ref.shape[0]):
        rows = slice(slot * 8, slot * 8 + 8)
        alpha = alpha_ref[source_ref[slot]]
        total = total + alpha[:8, :1] * first_ref[rows, :] + alpha[8:, :1] * second_ref[rows, :]
    out_ref[...] = total


def whole(shape):
    return pl.BlockSpec(shape, lambda i, *_: (0,) * len(shape))


SMEM = pl.BlockSpec(memory_space=pltpu.SMEM)
VMEM_LIMIT = 48 * 1024 * 1024


def cost(microseconds):
    return pl.CostEstimate(
        flops=int(microseconds * 1e9), bytes_accessed=1000, transcendentals=0
    )


def params(**kw):
    return pltpu.CompilerParams(vmem_limit_bytes=VMEM_LIMIT, **kw)


def on_plane(positions, panel_area, self_term, excitation, adjacency, block_list, block_count):
    count = excitation.shape[2]
    subs = adjacency.shape[0]
    ranks = subs
    unknowns = count * ranks
    scale = 1.0 / math.sqrt(unknowns)
    tiles = count // TILE
    half = count // 2
    own_width = (tiles // 2 + 1) * TILE
    plane = lax.axis_index("row")
    place = lax.axis_index("sub")

    swap = [(z * subs + s, s * subs + z) for z in range(ranks) for s in range(subs)]

    def over(bit):
        return [(s, s ^ bit) for s in range(subs)]

    def send(x, bit):
        return lax.ppermute(x, "sub", over(bit))

    pack = jnp.concatenate(
        [
            positions[0],
            panel_area,
            self_term,
            jnp.zeros((3, count), F32),
            excitation[0],
        ],
        axis=0,
    )
    pack = lax.ppermute(pack, ("row", "sub"), swap)

    mine = jnp.arange(subs, dtype=jnp.int32) == plane
    neighbours = jnp.sum(jnp.where(mine[:, None], adjacency, 0), axis=0)
    lists = jnp.sum(jnp.where(mine[:, None, None], block_list, 0), axis=0)
    counts = jnp.sum(jnp.where(mine[:, None], block_count, 0), axis=0)
    source = jnp.maximum((plane - neighbours + subs) % subs - 1, 0)
    first_block = (place * (count // BLK)).astype(jnp.int32).reshape(1)

    def from_planes(x):
        got = []
        for k in range(1, ranks):
            shift = [(z, (z + k) % ranks) for z in range(ranks)]
            got.append(lax.ppermute(x, "row", shift))
        return jnp.stack(got)

    far = from_planes(pack)

    f32 = lambda *s: jax.ShapeDtypeStruct(s, F32)
    b16 = lambda *s: jax.ShapeDtypeStruct(s, BF16)
    fp8 = lambda *s: jax.ShapeDtypeStruct(s, FP8)

    left, right_own, field_own, small_own, undo_own = pl.pallas_call(
        functools.partial(prep_kernel, scale, True),
        out_shape=(
            b16(count, 128),
            b16(FEATURES, 2 * count),
            b16(16, 2 * count),
            fp8(8, 2 * count),
            f32(8, 128),
        ),
        compiler_params=params(),
        name="prep_own",
    )(pack)

    pack2 = send(pack, 2)
    packs = jnp.stack([pack, pack2])
    packs_odd = send(packs, 1)
    full = jnp.concatenate([pack, packs_odd[0], pack2, packs_odd[1]], axis=1)

    build_own = pl.pallas_call(
        build_own_kernel,
        grid=(tiles,),
        in_specs=[
            whole((count, 128)),
            whole((FEATURES, 2 * count)),
            whole((16, 2 * count)),
            whole((8, 2 * count)),
            whole((8, 128)),
        ],
        out_specs=(
            pl.BlockSpec((TILE, own_width), lambda i: (i, 0)),
            pl.BlockSpec((TILE, own_width), lambda i: (i, 0)),
            whole((8, 2 * count)),
        ),
        out_shape=(b16(count, own_width), fp8(count, own_width), f32(8, 2 * count)),
        scratch_shapes=[pltpu.VMEM((TILE, own_width), F32)],
        compiler_params=params(),
        cost_estimate=cost(17),
        name="build_own",
    )
    own_high, own_low, acc = build_own(left, right_own, field_own, small_own, undo_own)

    others = []
    for b in range(1, 4):
        others.append(
            pl.pallas_call(
                lambda p, *outs: prep_kernel(scale, False, p, None, *outs),
                out_shape=(b16(FEATURES, count), b16(16, count), fp8(8, count), f32(8, 128)),
                compiler_params=params(),
                name="prep_oth",
            )(full[:, b * count : (b + 1) * count])
        )
    right_oth, field_oth, small_oth, undo_oth = (
        jnp.concatenate(parts, axis=1) for parts in zip(*others)
    )

    parity = jnp.stack([(place > (place ^ b)).astype(jnp.int32) for b in range(1, 4)])

    oth_high, oth_low, part = pl.pallas_call(
        build_oth_kernel,
        grid_spec=pltpu.PrefetchScalarGridSpec(
            num_scalar_prefetch=1,
            grid=(tiles,),
            in_specs=[
                whole((count, 128)),
                whole((FEATURES, 3 * count)),
                whole((16, 2 * count)),
                whole((8, 2 * count)),
                whole((8, 128)),
                whole((16, 3 * count)),
                whole((8, 3 * count)),
                whole((8, 3 * 128)),
                whole((8, 2 * count)),
                pl.BlockSpec(memory_space=pl.ANY),
            ],
            out_specs=(
                pl.BlockSpec((TILE, 3 * half), lambda i, *_: (i, 0)),
                pl.BlockSpec((TILE, 3 * half), lambda i, *_: (i, 0)),
                whole((8, 4 * count)),
            ),
            scratch_shapes=[
                pltpu.VMEM((2, TILE, half), F32),
                pltpu.VMEM((8, 2 * count), F32),
                pltpu.VMEM((8, 3 * count), F32),
            ],
        ),
        out_shape=(b16(count, 3 * half), fp8(count, 3 * half), f32(8, 4 * count)),
        compiler_params=params(),
        cost_estimate=cost(42),
        name="build_oth",
    )(
        parity, left, right_oth, field_own, small_own, undo_own,
        field_oth, small_oth, undo_oth, acc, far,
    )

    def pair(x, a, b):
        return jnp.concatenate(
            [x[:, a * count : (a + 1) * count], x[:, b * count : (b + 1) * count]], axis=1
        )

    def reduce_all(part):
        got = send(pair(part, 1, 3), 1)
        chip = pair(part, 0, 2) + got
        got = send(chip, 2)
        even = chip + pair(got, 1, 0)
        odd = send(even, 1)
        return even, odd

    def apply(res):
        own_spec = pl.BlockSpec((TILE, own_width), lambda i, *_: (i, 0))
        oth_spec = pl.BlockSpec((TILE, 3 * half), lambda i, *_: (i, 0))
        return pl.pallas_call(
            functools.partial(apply_kernel, scale),
            grid_spec=pltpu.PrefetchScalarGridSpec(
                num_scalar_prefetch=1,
                grid=(tiles,),
                in_specs=[
                    whole((16, 4 * count)),
                    whole((8, 4 * count)),
                    own_spec,
                    own_spec,
                    oth_spec,
                    oth_spec,
                ],
                out_specs=whole((8, 4 * count)),
                scratch_shapes=[
                    pltpu.VMEM((16, 2 * count), BF16),
                    pltpu.VMEM((16, 3 * count), BF16),
                    pltpu.VMEM((8, 2 * count), FP8),
                    pltpu.VMEM((8, 3 * count), FP8),
                    pltpu.VMEM((8, 4 * 128), F32),
                    pltpu.VMEM((8, 2 * count), F32),
                    pltpu.VMEM((8, 3 * count), F32),
                ],
            ),
            out_shape=f32(8, 4 * count),
            compiler_params=params(),
            cost_estimate=cost(22),
            name="apply",
        )(parity, full, res, own_high, own_low, oth_high, oth_low)

    def step(part, res, *cur):
        even, odd = reduce_all(part)
        return pl.pallas_call(
            step_kernel,
            out_shape=[f32(8, 4 * count)] * 2 + [f32(8, 128)],
            compiler_params=params(),
            name="step",
        )(even, odd, full, res, *cur)

    slots = adjacency.shape[1]
    vmem = pl.BlockSpec(memory_space=pltpu.VMEM)
    tile_high, tile_low, weight, first_part = pl.pallas_call(
        couple_kernel,
        in_specs=[SMEM] * 4 + [vmem] * 2,
        out_shape=(
            b16(slots, count, 128),
            b16(slots, count, 128),
            f32(8 * slots, count),
            f32(8 * slots, count),
        ),
        compiler_params=params(),
        cost_estimate=cost(4),
        name="couple",
    )(source, lists, counts, first_block, pack, far)

    res, cur, alpha_first = step(part, full[8:])
    far_res = from_planes(res[:, :count])
    part = apply(res)
    second_part = pl.pallas_call(
        couple_again_kernel,
        in_specs=[SMEM] + [vmem] * 4,
        out_shape=f32(8 * slots, count),
        compiler_params=params(),
        cost_estimate=cost(1),
        name="couple_again",
    )(source, tile_high, tile_low, weight, far_res)
    res, cur, alpha_second = step(part, res, cur)
    coupled = pl.pallas_call(
        combine_kernel,
        in_specs=[SMEM] + [vmem] * 3,
        out_shape=f32(8, count),
        compiler_params=params(),
        name="combine",
    )(
        source,
        from_planes(jnp.concatenate([alpha_first, alpha_second], axis=0)),
        first_part,
        second_part,
    )
    coupled_across = send(coupled, 2)
    odd = send(jnp.concatenate([coupled, coupled_across], axis=1), 1)
    res = res - jnp.concatenate(
        [coupled, odd[:, :count], coupled_across, odd[:, count:]], axis=1
    )

    res, cur, _ = step(apply(res), res, cur)
    res, cur, _ = step(apply(res), res, cur)
    out = jnp.concatenate([cur[:, :count], res[:, :count]], axis=0)
    out = lax.ppermute(out, ("row", "sub"), swap)
    return out[None, :8], out[None, 8:]


def kernel_tile(near, far, area, scale):
    squared = jnp.zeros(near.shape[1:] + far.shape[-1:], jnp.float32)
    for coord in range(3):
        spacing = near[coord][..., :, None] - far[coord][..., None, :]
        squared = squared + spacing * spacing
    radius = jnp.sqrt(squared)
    return jnp.cos(KAPPA * radius) / (1.0 + radius) * (area * scale)[..., None, :]


def pick_source(table, chosen):
    shaped = chosen.reshape(chosen.shape + (1,) * (table.ndim - 1))
    return jnp.sum(jnp.where(shaped, table, jnp.zeros_like(table)), axis=0)


def on_rows(positions, panel_area, self_term, excitation, adjacency, block_list, block_count):
    width = excitation.shape[1]
    rows_here = excitation.shape[2]
    near = positions[0]
    diagonal = self_term[0]
    gathered_pos, gathered_area = (
        lax.all_gather(positions[0], "row", axis=1, tiled=True),
        lax.all_gather(panel_area[0], "row", axis=0, tiled=True),
    )
    other_pos, other_area = (
        lax.all_gather(positions, "sub", axis=0, tiled=True),
        lax.all_gather(panel_area, "sub", axis=0, tiled=True),
    )
    total_cols = gathered_pos.shape[1]
    scale = 1.0 / math.sqrt(total_cols)
    subdomains = adjacency.shape[0]
    local_blocks = rows_here // BLK

    def build_step(counter, stored):
        offset = counter * column_block
        block_pos = lax.dynamic_slice_in_dim(gathered_pos, offset, column_block, 1)
        block_area = lax.dynamic_slice_in_dim(gathered_area, offset, column_block, 0)
        tile = kernel_tile(near, block_pos, block_area, scale)
        return lax.dynamic_update_slice_in_dim(stored, tile, offset, 1)

    self_rows = lax.fori_loop(
        0, total_cols // column_block, build_step, jnp.zeros((rows_here, total_cols), jnp.float32)
    )

    def apply_self(field):
        product = lax.dot_general(
            lax.all_gather(field[None], "row", axis=2, tiled=True)[0],
            self_rows,
            (((1,), (1,)), ((), ())),
            precision=lax.Precision.HIGHEST,
            preferred_element_type=jnp.float32,
        )
        return diagonal[None, :] * field + product

    currents = jnp.zeros((width, rows_here), jnp.float32)
    residual = excitation[0]
    for outer_step in range(OUTER):
        if outer_step > 0:
            all_currents = lax.all_gather(currents[None], "sub", axis=0, tiled=True)
            mine = jnp.arange(subdomains, dtype=jnp.int32) == lax.axis_index("sub")
            my_adjacency = jnp.sum(jnp.where(mine[:, None], adjacency, 0), axis=0)
            my_lists = jnp.sum(jnp.where(mine[:, None, None], block_list, 0), axis=0)
            my_counts = jnp.sum(jnp.where(mine[:, None], block_count, 0), axis=0)
            first_block = lax.axis_index("row") * local_blocks
            global_ids = first_block + jnp.arange(local_blocks, dtype=jnp.int32)
            total = jnp.zeros((width, local_blocks, BLK), jnp.float32)
            for slot in range(adjacency.shape[1]):
                chosen = jnp.arange(subdomains, dtype=jnp.int32) == my_adjacency[slot]
                src_pos = pick_source(other_pos, chosen)
                src_area = pick_source(other_area, chosen)
                src_cur = pick_source(all_currents, chosen)
                tiles = kernel_tile(
                    near.reshape(3, local_blocks, BLK),
                    src_pos.reshape(3, local_blocks, BLK),
                    src_area.reshape(local_blocks, BLK),
                    COUPLE / math.sqrt(BLK),
                )
                coupling_product = jnp.einsum(
                    "bpq,ebq->ebp",
                    tiles,
                    src_cur.reshape(width, local_blocks, BLK),
                    precision=lax.Precision.HIGHEST,
                )
                listed = (my_lists[slot][:, None] == global_ids[None, :]) & (
                    jnp.arange(my_lists.shape[1], dtype=jnp.int32)[:, None] < my_counts[slot]
                )
                weight = jnp.sum(listed.astype(jnp.float32), axis=0)
                total = total + coupling_product * weight[None, :, None]
            coupled = total.reshape(width, rows_here)
            residual = residual - coupled
        image = apply_self(residual)
        second = apply_self(image)
        cross, square, res_second, img_second, sec_second = lax.psum(
            (
                jnp.sum(residual * image, axis=1),
                jnp.sum(image * image, axis=1),
                jnp.sum(residual * second, axis=1),
                jnp.sum(image * second, axis=1),
                jnp.sum(second * second, axis=1),
            ),
            "row",
        )
        first_alpha = cross / (square + EPS)
        currents = currents + first_alpha[:, None] * residual
        residual = residual - first_alpha[:, None] * image
        image = image - first_alpha[:, None] * second
        cross_next = (
            cross
            - first_alpha * res_second
            - first_alpha * square
            + first_alpha * first_alpha * img_second
        )
        square_next = (
            square - 2.0 * first_alpha * img_second + first_alpha * first_alpha * sec_second
        )
        next_alpha = cross_next / (square_next + EPS)
        currents = currents + next_alpha[:, None] * residual
        residual = residual - next_alpha[:, None] * image
    return (currents[None], residual[None])


def on_device(sizes, *arrays):
    excitation, adjacency = arrays[3], arrays[4]
    count = excitation.shape[2]
    square = sizes["row"] == sizes["sub"] == adjacency.shape[0] == 4
    if square and excitation.shape[1] == 8 and count % (2 * TILE) == 0:
        return on_plane(*arrays)
    return on_rows(*arrays)


def solution(mesh):
    in_specs = (
        P(("body", "sub"), None, "row"),
        P(("body", "sub"), "row"),
        P(("body", "sub"), "row"),
        P(("body", "sub"), None, "row"),
        P("body", None),
        P("body", None, None),
        P("body", None),
    )
    out_specs = (P(("body", "sub"), None, "row"), P(("body", "sub"), None, "row"))
    sizes = {name: mesh.shape[name] for name in ("row", "sub")}
    step = jax.shard_map(
        functools.partial(on_device, sizes),
        mesh=mesh,
        in_specs=in_specs,
        out_specs=out_specs,
        check_vma=False,
    )
    if sizes["row"] != sizes["sub"]:
        return step
    return step
```

```python
import functools
import math

import jax
import jax.numpy as jnp
from jax import lax
from jax.experimental import pallas as pl
from jax.experimental.pallas import tpu as pltpu
from jax.sharding import PartitionSpec as P


BLK = 32
OUTER = 2

KAPPA = 40.0
COUPLE = 1.0
EPS = 1e-06
column_block = 2048

F32 = jnp.float32
BF16 = jnp.bfloat16
TILE = 256
CHUNK = 32
FEATURES = 96
WAVE = KAPPA / (2.0 * math.pi)
ROUNDER = 12582912.0
HALF_COSINE = (
    0.9999982896004456,
    -4.934458936893249,
    4.048771939331772,
    -1.2478000348360374,
)
LIFT = 65536.0
FP8 = jnp.float8_e4m3fn
FP8_PEAK = 224.0


def to_grid(x, step):
    shift = ROUNDER * step
    return (x + shift) - shift


def cos_and_one(turns, amplitude):
    u = turns - jnp.round(turns)
    s = u * u
    factor = math.sqrt(2.0 * amplitude)
    value = HALF_COSINE[-1] * factor
    for coefficient in HALF_COSINE[-2::-1]:
        value = value * s + coefficient * factor
    return value * value


def green(squared_turns):
    y = jnp.maximum(squared_turns, 1e-12)
    turns = y * lax.rsqrt(y)
    amplitude = WAVE * LIFT
    return (cos_and_one(turns, amplitude) - amplitude) / (turns + WAVE)


def features(points):
    row = lax.broadcasted_iota(jnp.int32, points.shape, 0)
    centred = jnp.where(row < 3, (points - 0.5) * WAVE, 0.0)
    high = to_grid(centred, 2.0**-6)
    rest = centred - high
    mid = to_grid(rest, 2.0**-14)
    low = rest - mid
    coarse = jnp.sum(high * high, axis=0, keepdims=True)
    fine = jnp.sum(2.0 * high * rest + rest * rest, axis=0, keepdims=True)
    a = to_grid(coarse, 0.25)
    b = to_grid(coarse - a, 2.0**-10)
    c = coarse - a - b
    d = fine.astype(BF16).astype(F32)
    e = (fine - d).astype(BF16).astype(F32)
    f = fine - d - e
    norm = jnp.zeros_like(centred)
    for k, piece in enumerate((a, b, c, d, e, f)):
        norm = jnp.where(row == k, piece, norm)
    one = jnp.where(row < 6, 1.0, 0.0)
    zero = jnp.zeros_like(centred)
    left = (high, norm, one, high, mid, high, low, mid, mid, low, low, zero)
    right = (high, one, norm, mid, high, low, high, mid, low, mid, low, zero)
    right = tuple(-2.0 * x if k not in (1, 2) else x for k, x in enumerate(right))
    return left, right


def two_pieces(x):
    high = x.astype(BF16).astype(F32)
    return jnp.concatenate([high, x - high], axis=0).astype(BF16)


def fp8_piece(x):
    peak = jnp.maximum(jnp.max(jnp.abs(x), axis=1, keepdims=True), 1e-30)
    return (x * (FP8_PEAK / peak)).astype(FP8), peak * (1.0 / FP8_PEAK)


def nn(left, right):
    return lax.dot_general(left, right, (((1,), (0,)), ((), ())), preferred_element_type=F32)


def nt(left, right):
    return lax.dot_general(left, right, (((1,), (1,)), ((), ())), preferred_element_type=F32)


def pack_kernel(positions_ref, area_ref, term_ref, excitation_ref, pack_ref):
    pack_ref[0:3, :] = positions_ref[0]
    pack_ref[3:4, :] = area_ref[...]
    pack_ref[4:5, :] = term_ref[...]
    pack_ref[5:8, :] = jnp.zeros((3, pack_ref.shape[1]), F32)
    pack_ref[8:16, :] = excitation_ref[0]


def prep_kernel(scale, doubled, pack_ref, left_ref, right_ref, field_ref, small_ref, undo_ref):
    pack = pack_ref[...]
    count = pack.shape[1]
    left, right = features(pack[:8])
    right = jnp.concatenate(right, axis=0).astype(BF16)
    weighted = pack[8:] * (pack[3:4] * (scale / LIFT))
    field = two_pieces(weighted)
    small, undo = fp8_piece(weighted)
    undo_ref[...] = jnp.broadcast_to(undo, undo_ref.shape)
    if doubled:
        for k in range(2):
            right_ref[:, k * count : (k + 1) * count] = right
            field_ref[:, k * count : (k + 1) * count] = field
            small_ref[:, k * count : (k + 1) * count] = small
        left = jnp.concatenate(left + (jnp.zeros((128 - FEATURES, count), F32),), axis=0)
        for k in range(count // TILE):
            left_ref[k * TILE : (k + 1) * TILE, :] = left[:, k * TILE : (k + 1) * TILE].T.astype(BF16)
    else:
        half = count // 2
        for k in range(count // TILE):
            to = (k % 2) * half + (k // 2) * TILE
            right_ref[:, to : to + TILE] = right[:, k * TILE : (k + 1) * TILE]
            field_ref[:, to : to + TILE] = field[:, k * TILE : (k + 1) * TILE]
            small_ref[:, to : to + TILE] = small[:, k * TILE : (k + 1) * TILE]


def fill_tile(source, at, target_high, target_low, to):
    for c in range(TILE // CHUNK):
        rows = slice(c * CHUNK, (c + 1) * CHUNK)
        g = green(source[rows, at : at + TILE])
        high = g.astype(BF16)
        target_high[rows, to : to + TILE] = high
        target_low[rows, to : to + TILE] = (g - high.astype(F32)).astype(FP8)


def fold_pieces(x):
    return x[:8] + x[8:]


def build_own_kernel(
    left_ref, right_ref, field_ref, small_ref, undo_ref, high_ref, low_ref, acc_ref, dist
):
    i = pl.program_id(0)
    width = high_ref.shape[1]
    tiles = width // TILE
    here = pl.multiple_of(i * TILE, TILE)

    @pl.when(i == 0)
    def _():
        acc_ref[...] = jnp.zeros_like(acc_ref)

    dist[...] = nn(
        left_ref[pl.ds(here, TILE), :FEATURES], right_ref[:, pl.ds(here, width)]
    )
    mine = field_ref[:, pl.ds(here, TILE)]
    mine_small = small_ref[:, pl.ds(here, TILE)]
    undo = undo_ref[:, :1]
    total = jnp.zeros((8, TILE), F32)
    for k in range(tiles):
        fill_tile(dist, k * TILE, high_ref, low_ref, k * TILE)
        there = pl.ds(pl.multiple_of(here + k * TILE, TILE), TILE)
        high = high_ref[:, k * TILE : (k + 1) * TILE]
        low = low_ref[:, k * TILE : (k + 1) * TILE]
        total += fold_pieces(nt(field_ref[:, there], high)) + nt(small_ref[:, there], low) * undo
        if 0 < k < tiles - 1:
            acc_ref[:, there] += fold_pieces(nn(mine, high)) + nn(mine_small, low) * undo
    acc_ref[:, pl.ds(here, TILE)] += total


def write_partial(part_ref, acc_own, acc_oth):
    count = acc_own.shape[1] // 2
    half = count // 2
    part_ref[:, :count] = acc_own[:, :count] + acc_own[:, count:]
    for b in range(3):
        for k in range(count // TILE):
            at = b * count + (k % 2) * half + (k // 2) * TILE
            to = (b + 1) * count + k * TILE
            part_ref[:, to : to + TILE] = acc_oth[:, at : at + TILE]


def build_oth_kernel(
    parity_ref, left_ref, right_ref, own_ref, own_small_ref, own_undo_ref,
    field_ref, small_ref, undo_ref, acc_in_ref,
    high_ref, low_ref, part_ref, dist, acc_own, acc_oth,
):
    i = pl.program_id(0)
    count = left_ref.shape[0]
    half = count // 2
    tiles = half // TILE
    here = pl.multiple_of(i * TILE, TILE)

    @pl.when(i == 0)
    def _():
        acc_own[...] = acc_in_ref[...]
        acc_oth[...] = jnp.zeros_like(acc_oth)

    offsets = [
        pl.multiple_of(b * count + ((i + parity_ref[b]) & 1) * half, TILE) for b in range(3)
    ]
    left = left_ref[pl.ds(here, TILE), :FEATURES]
    mine = own_ref[:, pl.ds(here, TILE)]
    mine_small = own_small_ref[:, pl.ds(here, TILE)]
    mine_undo = own_undo_ref[:, :1]
    total = jnp.zeros((8, TILE), F32)
    dist[0] = nn(left, right_ref[:, pl.ds(offsets[0], half)])
    for b in range(3):
        if b < 2:
            dist[(b + 1) % 2] = nn(left, right_ref[:, pl.ds(offsets[b + 1], half)])
        undo = undo_ref[:, b * 128 : b * 128 + 1]
        for k in range(tiles):
            to = b * half + k * TILE
            fill_tile(dist.at[b % 2], k * TILE, high_ref, low_ref, to)
            there = pl.ds(pl.multiple_of(offsets[b] + k * TILE, TILE), TILE)
            high = high_ref[:, to : to + TILE]
            low = low_ref[:, to : to + TILE]
            total += fold_pieces(nt(field_ref[:, there], high)) + nt(small_ref[:, there], low) * undo
            acc_oth[:, there] += fold_pieces(nn(mine, high)) + nn(mine_small, low) * mine_undo
    acc_own[:, pl.ds(here, TILE)] += total

    @pl.when(i == pl.num_programs(0) - 1)
    def _():
        write_partial(part_ref, acc_own, acc_oth)


def step_kernel(even_ref, odd_ref, pack_ref, res_ref, *refs):
    cur_ref = refs[0] if len(refs) == 4 else None
    new_res_ref, new_cur_ref, alpha_ref = refs[-3:]
    count = even_ref.shape[1] // 2
    numerator = 0.0
    denominator = 0.0
    for b in range(4):
        source = odd_ref if b % 2 else even_ref
        product = source[:, (b // 2) * count : (b // 2 + 1) * count]
        cols = slice(b * count, (b + 1) * count)
        res = res_ref[:, cols]
        img = pack_ref[4:5, cols] * res + product
        new_res_ref[:, cols] = img
        numerator = numerator + jnp.sum(res * img, axis=1, keepdims=True)
        denominator = denominator + jnp.sum(img * img, axis=1, keepdims=True)
    alpha = numerator / (denominator + EPS)
    alpha_ref[...] = jnp.broadcast_to(alpha, alpha_ref.shape)
    for b in range(4):
        cols = slice(b * count, (b + 1) * count)
        res = res_ref[:, cols]
        if cur_ref is None:
            new_cur_ref[:, cols] = alpha * res
        else:
            new_cur_ref[:, cols] = cur_ref[:, cols] + alpha * res
        new_res_ref[:, cols] = res - alpha * new_res_ref[:, cols]


def apply_kernel(
    scale, parity_ref, pack_ref, res_ref, own_high, own_low, oth_high, oth_low,
    part_ref, own_field, oth_field, own_small, oth_small, undos, acc_own, acc_oth,
):
    i = pl.program_id(0)
    count = res_ref.shape[1] // 4
    half = count // 2
    here = pl.multiple_of(i * TILE, TILE)

    @pl.when(i == 0)
    def _():
        acc_own[...] = jnp.zeros_like(acc_own)
        acc_oth[...] = jnp.zeros_like(acc_oth)
        for b in range(4):
            cols = slice(b * count, (b + 1) * count)
            weighted = res_ref[:, cols] * (pack_ref[3:4, cols] * (scale / LIFT))
            field = two_pieces(weighted)
            small, undo = fp8_piece(weighted)
            undos[:, b * 128 : (b + 1) * 128] = jnp.broadcast_to(undo, (8, 128))
            if b == 0:
                for k in range(2):
                    own_field[:, k * count : (k + 1) * count] = field
                    own_small[:, k * count : (k + 1) * count] = small
                continue
            for k in range(count // TILE):
                to = (b - 1) * count + (k % 2) * half + (k // 2) * TILE
                oth_field[:, to : to + TILE] = field[:, k * TILE : (k + 1) * TILE]
                oth_small[:, to : to + TILE] = small[:, k * TILE : (k + 1) * TILE]

    width = own_high.shape[1]
    mine = own_field[:, pl.ds(here, TILE)]
    mine_small = own_small[:, pl.ds(here, TILE)]
    undo = undos[:, :1]
    span = pl.ds(here, width)
    inner = pl.ds(pl.multiple_of(here + TILE, TILE), width - 2 * TILE)
    total = fold_pieces(nt(own_field[:, span], own_high[...]))
    total += nt(own_small[:, span], own_low[...]) * undo
    acc_own[:, inner] += (
        fold_pieces(nn(mine, own_high[:, TILE : width - TILE]))
        + nn(mine_small, own_low[:, TILE : width - TILE]) * undo
    )
    for b in range(3):
        there = pl.ds(
            pl.multiple_of(b * count + ((i + parity_ref[b]) & 1) * half, TILE), half
        )
        high = oth_high[:, b * half : (b + 1) * half]
        low = oth_low[:, b * half : (b + 1) * half]
        total += fold_pieces(nt(oth_field[:, there], high))
        total += nt(oth_small[:, there], low) * undos[:, (b + 1) * 128 : (b + 1) * 128 + 1]
        acc_oth[:, there] += fold_pieces(nn(mine, high)) + nn(mine_small, low) * undo
    acc_own[:, pl.ds(here, TILE)] += total

    @pl.when(i == pl.num_programs(0) - 1)
    def _():
        write_partial(part_ref, acc_own, acc_oth)


def interface_product(field, high, low):
    pieces = two_pieces(field)
    return fold_pieces(nt(pieces, high) + nt(pieces, low))


def couple_kernel(
    source_ref, list_ref, count_ref, first_ref, near_ref, far_ref,
    high_ref, low_ref, weight_ref, out_ref,
):
    count = near_ref.shape[1]
    slots = count_ref.shape[0]
    lane = lax.broadcasted_iota(jnp.int32, (1, count), 1)
    ident = first_ref[0] + lane // BLK
    row = lax.broadcasted_iota(jnp.int32, (128, 128), 0) // BLK
    col = lax.broadcasted_iota(jnp.int32, (128, 128), 1) // BLK
    same = row == col
    for slot in range(slots):
        hits = jnp.zeros((1, count), F32)
        for k in range(list_ref.shape[1]):
            hit = (ident == list_ref[slot, k]) & (k < count_ref[slot])
            hits = hits + jnp.where(hit, 1.0, 0.0)
        weight_ref[slot * 8 : slot * 8 + 8, :] = jnp.broadcast_to(hits, (8, count))
    for g in range(count // 128):
        cols = slice(g * 128, (g + 1) * 128)
        near = near_ref[:8, cols].T
        for slot in range(slots):
            far = far_ref[source_ref[slot], :, cols]
            squared = jnp.zeros((128, 128), F32)
            for x in range(3):
                gap = near[:, x : x + 1] - far[x : x + 1, :]
                squared = squared + gap * gap
            safe = jnp.maximum(squared, 1e-30)
            radius = safe * lax.rsqrt(safe)
            tile = (cos_and_one(radius * WAVE, 1.0) - 1.0) / (1.0 + radius)
            tile = jnp.where(same, tile * (far[3:4, :] * (COUPLE / math.sqrt(BLK))), 0.0)
            high = tile.astype(BF16)
            low = (tile - high.astype(F32)).astype(BF16)
            high_ref[slot, cols, :] = high
            low_ref[slot, cols, :] = low
            rows = slice(slot * 8, slot * 8 + 8)
            out_ref[rows, cols] = interface_product(far[8:], high, low) * weight_ref[rows, cols]


def couple_again_kernel(source_ref, high_ref, low_ref, weight_ref, far_ref, out_ref):
    for g in range(out_ref.shape[1] // 128):
        cols = slice(g * 128, (g + 1) * 128)
        for slot in range(source_ref.shape[0]):
            rows = slice(slot * 8, slot * 8 + 8)
            far = far_ref[source_ref[slot], :, cols]
            product = interface_product(far, high_ref[slot, cols, :], low_ref[slot, cols, :])
            out_ref[rows, cols] = product * weight_ref[rows, cols]


def combine_kernel(source_ref, alpha_ref, first_ref, second_ref, out_ref):
    total = 0.0
    for slot in range(source_ref.shape[0]):
        rows = slice(slot * 8, slot * 8 + 8)
        alpha = alpha_ref[source_ref[slot]]
        total = total + alpha[:8, :1] * first_ref[rows, :] + alpha[8:, :1] * second_ref[rows, :]
    out_ref[...] = total


def whole(shape):
    return pl.BlockSpec(shape, lambda i, *_: (0,) * len(shape))


SMEM = pl.BlockSpec(memory_space=pltpu.SMEM)
VMEM_LIMIT = 48 * 1024 * 1024


def cost(microseconds):
    return pl.CostEstimate(
        flops=int(microseconds * 1e9), bytes_accessed=1000, transcendentals=0
    )


def params(**kw):
    return pltpu.CompilerParams(vmem_limit_bytes=VMEM_LIMIT, **kw)


def on_plane(positions, panel_area, self_term, excitation, adjacency, block_list, block_count):
    count = excitation.shape[2]
    subs = adjacency.shape[0]
    ranks = subs
    unknowns = count * ranks
    scale = 1.0 / math.sqrt(unknowns)
    tiles = count // TILE
    half = count // 2
    own_width = (tiles // 2 + 1) * TILE
    plane = lax.axis_index("row")
    place = lax.axis_index("sub")

    swap = [(z * subs + s, s * subs + z) for z in range(ranks) for s in range(subs)]

    def over(bit):
        return [(s, s ^ bit) for s in range(subs)]

    def send(x, bit):
        return lax.ppermute(x, "sub", over(bit))

    pack = pl.pallas_call(
        pack_kernel,
        out_shape=jax.ShapeDtypeStruct((16, count), F32),
        compiler_params=params(),
        name="pack",
    )(positions, panel_area, self_term, excitation)
    pack = lax.ppermute(pack, ("row", "sub"), swap)

    mine = jnp.arange(subs, dtype=jnp.int32) == plane
    neighbours = jnp.sum(jnp.where(mine[:, None], adjacency, 0), axis=0)
    lists = jnp.sum(jnp.where(mine[:, None, None], block_list, 0), axis=0)
    counts = jnp.sum(jnp.where(mine[:, None], block_count, 0), axis=0)
    source = jnp.maximum((plane - neighbours + subs) % subs - 1, 0)
    first_block = (place * (count // BLK)).astype(jnp.int32).reshape(1)

    def from_planes(x):
        got = []
        for k in range(1, ranks):
            shift = [(z, (z + k) % ranks) for z in range(ranks)]
            got.append(lax.ppermute(x, "row", shift))
        return jnp.stack(got)

    far = from_planes(pack)

    f32 = lambda *s: jax.ShapeDtypeStruct(s, F32)
    b16 = lambda *s: jax.ShapeDtypeStruct(s, BF16)
    fp8 = lambda *s: jax.ShapeDtypeStruct(s, FP8)

    left, right_own, field_own, small_own, undo_own = pl.pallas_call(
        functools.partial(prep_kernel, scale, True),
        out_shape=(
            b16(count, 128),
            b16(FEATURES, 2 * count),
            b16(16, 2 * count),
            fp8(8, 2 * count),
            f32(8, 128),
        ),
        compiler_params=params(),
        name="prep_own",
    )(pack)

    blocks = [pack]
    for bit in range(1, subs):
        blocks.append(send(pack, bit))
    full = jnp.concatenate(blocks, axis=1)

    build_own = pl.pallas_call(
        build_own_kernel,
        grid=(tiles,),
        in_specs=[
            whole((count, 128)),
            whole((FEATURES, 2 * count)),
            whole((16, 2 * count)),
            whole((8, 2 * count)),
            whole((8, 128)),
        ],
        out_specs=(
            pl.BlockSpec((TILE, own_width), lambda i: (i, 0)),
            pl.BlockSpec((TILE, own_width), lambda i: (i, 0)),
            whole((8, 2 * count)),
        ),
        out_shape=(b16(count, own_width), fp8(count, own_width), f32(8, 2 * count)),
        scratch_shapes=[pltpu.VMEM((TILE, own_width), F32)],
        compiler_params=params(),
        cost_estimate=cost(17),
        name="build_own",
    )
    own_high, own_low, acc = build_own(left, right_own, field_own, small_own, undo_own)

    others = []
    for b in range(1, 4):
        others.append(
            pl.pallas_call(
                lambda p, *outs: prep_kernel(scale, False, p, None, *outs),
                out_shape=(b16(FEATURES, count), b16(16, count), fp8(8, count), f32(8, 128)),
                compiler_params=params(),
                name="prep_oth",
            )(blocks[b])
        )
    right_oth, field_oth, small_oth, undo_oth = (
        jnp.concatenate(parts, axis=1) for parts in zip(*others)
    )

    parity = jnp.stack([(place > (place ^ b)).astype(jnp.int32) for b in range(1, 4)])

    build_oth = pl.pallas_call(
        build_oth_kernel,
        grid_spec=pltpu.PrefetchScalarGridSpec(
            num_scalar_prefetch=1,
            grid=(tiles,),
            in_specs=[
                whole((count, 128)),
                whole((FEATURES, 3 * count)),
                whole((16, 2 * count)),
                whole((8, 2 * count)),
                whole((8, 128)),
                whole((16, 3 * count)),
                whole((8, 3 * count)),
                whole((8, 3 * 128)),
                whole((8, 2 * count)),
            ],
            out_specs=(
                pl.BlockSpec((TILE, 3 * half), lambda i, *_: (i, 0)),
                pl.BlockSpec((TILE, 3 * half), lambda i, *_: (i, 0)),
                whole((8, 4 * count)),
            ),
            scratch_shapes=[
                pltpu.VMEM((2, TILE, half), F32),
                pltpu.VMEM((8, 2 * count), F32),
                pltpu.VMEM((8, 3 * count), F32),
            ],
        ),
        out_shape=(b16(count, 3 * half), fp8(count, 3 * half), f32(8, 4 * count)),
        compiler_params=params(),
        cost_estimate=cost(42),
        name="build_oth",
    )
    oth_high, oth_low, part = build_oth(
        parity, left, right_oth, field_own, small_own, undo_own,
        field_oth, small_oth, undo_oth, acc,
    )

    def pair(x, a, b):
        return jnp.concatenate(
            [x[:, a * count : (a + 1) * count], x[:, b * count : (b + 1) * count]], axis=1
        )

    def reduce_all(part):
        got = send(pair(part, 1, 3), 1)
        chip = pair(part, 0, 2) + got
        got = send(chip, 2)
        even = chip + pair(got, 1, 0)
        odd = send(even, 1)
        return even, odd

    def apply(res):
        own_spec = pl.BlockSpec((TILE, own_width), lambda i, *_: (i, 0))
        oth_spec = pl.BlockSpec((TILE, 3 * half), lambda i, *_: (i, 0))
        return pl.pallas_call(
            functools.partial(apply_kernel, scale),
            grid_spec=pltpu.PrefetchScalarGridSpec(
                num_scalar_prefetch=1,
                grid=(tiles,),
                in_specs=[
                    whole((16, 4 * count)),
                    whole((8, 4 * count)),
                    own_spec,
                    own_spec,
                    oth_spec,
                    oth_spec,
                ],
                out_specs=whole((8, 4 * count)),
                scratch_shapes=[
                    pltpu.VMEM((16, 2 * count), BF16),
                    pltpu.VMEM((16, 3 * count), BF16),
                    pltpu.VMEM((8, 2 * count), FP8),
                    pltpu.VMEM((8, 3 * count), FP8),
                    pltpu.VMEM((8, 4 * 128), F32),
                    pltpu.VMEM((8, 2 * count), F32),
                    pltpu.VMEM((8, 3 * count), F32),
                ],
            ),
            out_shape=f32(8, 4 * count),
            compiler_params=params(),
            cost_estimate=cost(22),
            name="apply",
        )(parity, full, res, own_high, own_low, oth_high, oth_low)

    def step(part, res, *cur):
        even, odd = reduce_all(part)
        return pl.pallas_call(
            step_kernel,
            out_shape=[f32(8, 4 * count)] * 2 + [f32(8, 128)],
            compiler_params=params(),
            name="step",
        )(even, odd, full, res, *cur)

    slots = adjacency.shape[1]
    vmem = pl.BlockSpec(memory_space=pltpu.VMEM)
    interface = pl.pallas_call(
        couple_kernel,
        in_specs=[SMEM] * 4 + [vmem] * 2,
        out_shape=(
            b16(slots, count, 128),
            b16(slots, count, 128),
            f32(8 * slots, count),
            f32(8 * slots, count),
        ),
        compiler_params=params(),
        cost_estimate=cost(4),
        name="couple",
    )
    tile_high, tile_low, weight, first_part = interface(
        source, lists, counts, first_block, pack, far
    )

    res, cur, alpha_first = step(part, full[8:])
    far_res = from_planes(res[:, :count])
    part = apply(res)
    second_part = pl.pallas_call(
        couple_again_kernel,
        in_specs=[SMEM] + [vmem] * 4,
        out_shape=f32(8 * slots, count),
        compiler_params=params(),
        cost_estimate=cost(1),
        name="couple_again",
    )(source, tile_high, tile_low, weight, far_res)
    res, cur, alpha_second = step(part, res, cur)
    coupled = pl.pallas_call(
        combine_kernel,
        in_specs=[SMEM] + [vmem] * 3,
        out_shape=f32(8, count),
        compiler_params=params(),
        name="combine",
    )(
        source,
        from_planes(jnp.concatenate([alpha_first, alpha_second], axis=0)),
        first_part,
        second_part,
    )
    coupled_across = send(coupled, 2)
    odd = send(jnp.concatenate([coupled, coupled_across], axis=1), 1)
    res = res - jnp.concatenate(
        [coupled, odd[:, :count], coupled_across, odd[:, count:]], axis=1
    )

    res, cur, _ = step(apply(res), res, cur)
    res, cur, _ = step(apply(res), res, cur)
    out = jnp.concatenate([cur[:, :count], res[:, :count]], axis=0)
    out = lax.ppermute(out, ("row", "sub"), swap)
    return out[None, :8], out[None, 8:]


def kernel_tile(near, far, area, scale):
    squared = jnp.zeros(near.shape[1:] + far.shape[-1:], jnp.float32)
    for coord in range(3):
        spacing = near[coord][..., :, None] - far[coord][..., None, :]
        squared = squared + spacing * spacing
    radius = jnp.sqrt(squared)
    return jnp.cos(KAPPA * radius) / (1.0 + radius) * (area * scale)[..., None, :]


def pick_source(table, chosen):
    shaped = chosen.reshape(chosen.shape + (1,) * (table.ndim - 1))
    return jnp.sum(jnp.where(shaped, table, jnp.zeros_like(table)), axis=0)


def on_rows(positions, panel_area, self_term, excitation, adjacency, block_list, block_count):
    width = excitation.shape[1]
    rows_here = excitation.shape[2]
    near = positions[0]
    diagonal = self_term[0]
    gathered_pos, gathered_area = (
        lax.all_gather(positions[0], "row", axis=1, tiled=True),
        lax.all_gather(panel_area[0], "row", axis=0, tiled=True),
    )
    other_pos, other_area = (
        lax.all_gather(positions, "sub", axis=0, tiled=True),
        lax.all_gather(panel_area, "sub", axis=0, tiled=True),
    )
    total_cols = gathered_pos.shape[1]
    scale = 1.0 / math.sqrt(total_cols)
    subdomains = adjacency.shape[0]
    local_blocks = rows_here // BLK

    def build_step(counter, stored):
        offset = counter * column_block
        block_pos = lax.dynamic_slice_in_dim(gathered_pos, offset, column_block, 1)
        block_area = lax.dynamic_slice_in_dim(gathered_area, offset, column_block, 0)
        tile = kernel_tile(near, block_pos, block_area, scale)
        return lax.dynamic_update_slice_in_dim(stored, tile, offset, 1)

    self_rows = lax.fori_loop(
        0, total_cols // column_block, build_step, jnp.zeros((rows_here, total_cols), jnp.float32)
    )

    def apply_self(field):
        product = lax.dot_general(
            lax.all_gather(field[None], "row", axis=2, tiled=True)[0],
            self_rows,
            (((1,), (1,)), ((), ())),
            precision=lax.Precision.HIGHEST,
            preferred_element_type=jnp.float32,
        )
        return diagonal[None, :] * field + product

    currents = jnp.zeros((width, rows_here), jnp.float32)
    residual = excitation[0]
    for outer_step in range(OUTER):
        if outer_step > 0:
            all_currents = lax.all_gather(currents[None], "sub", axis=0, tiled=True)
            mine = jnp.arange(subdomains, dtype=jnp.int32) == lax.axis_index("sub")
            my_adjacency = jnp.sum(jnp.where(mine[:, None], adjacency, 0), axis=0)
            my_lists = jnp.sum(jnp.where(mine[:, None, None], block_list, 0), axis=0)
            my_counts = jnp.sum(jnp.where(mine[:, None], block_count, 0), axis=0)
            first_block = lax.axis_index("row") * local_blocks
            global_ids = first_block + jnp.arange(local_blocks, dtype=jnp.int32)
            total = jnp.zeros((width, local_blocks, BLK), jnp.float32)
            for slot in range(adjacency.shape[1]):
                chosen = jnp.arange(subdomains, dtype=jnp.int32) == my_adjacency[slot]
                src_pos = pick_source(other_pos, chosen)
                src_area = pick_source(other_area, chosen)
                src_cur = pick_source(all_currents, chosen)
                tiles = kernel_tile(
                    near.reshape(3, local_blocks, BLK),
                    src_pos.reshape(3, local_blocks, BLK),
                    src_area.reshape(local_blocks, BLK),
                    COUPLE / math.sqrt(BLK),
                )
                coupling_product = jnp.einsum(
                    "bpq,ebq->ebp",
                    tiles,
                    src_cur.reshape(width, local_blocks, BLK),
                    precision=lax.Precision.HIGHEST,
                )
                listed = (my_lists[slot][:, None] == global_ids[None, :]) & (
                    jnp.arange(my_lists.shape[1], dtype=jnp.int32)[:, None] < my_counts[slot]
                )
                weight = jnp.sum(listed.astype(jnp.float32), axis=0)
                total = total + coupling_product * weight[None, :, None]
            coupled = total.reshape(width, rows_here)
            residual = residual - coupled
        image = apply_self(residual)
        second = apply_self(image)
        cross, square, res_second, img_second, sec_second = lax.psum(
            (
                jnp.sum(residual * image, axis=1),
                jnp.sum(image * image, axis=1),
                jnp.sum(residual * second, axis=1),
                jnp.sum(image * second, axis=1),
                jnp.sum(second * second, axis=1),
            ),
            "row",
        )
        first_alpha = cross / (square + EPS)
        currents = currents + first_alpha[:, None] * residual
        residual = residual - first_alpha[:, None] * image
        image = image - first_alpha[:, None] * second
        cross_next = (
            cross
            - first_alpha * res_second
            - first_alpha * square
            + first_alpha * first_alpha * img_second
        )
        square_next = (
            square - 2.0 * first_alpha * img_second + first_alpha * first_alpha * sec_second
        )
        next_alpha = cross_next / (square_next + EPS)
        currents = currents + next_alpha[:, None] * residual
        residual = residual - next_alpha[:, None] * image
    return (currents[None], residual[None])


def on_device(sizes, *arrays):
    excitation, adjacency = arrays[3], arrays[4]
    count = excitation.shape[2]
    square = sizes["row"] == sizes["sub"] == adjacency.shape[0] == 4
    if square and excitation.shape[1] == 8 and count % (2 * TILE) == 0:
        return on_plane(*arrays)
    return on_rows(*arrays)


def solution(mesh):
    in_specs = (
        P(("body", "sub"), None, "row"),
        P(("body", "sub"), "row"),
        P(("body", "sub"), "row"),
        P(("body", "sub"), None, "row"),
        P("body", None),
        P("body", None, None),
        P("body", None),
    )
    out_specs = (P(("body", "sub"), None, "row"), P(("body", "sub"), None, "row"))
    sizes = {name: mesh.shape[name] for name in ("row", "sub")}
    step = jax.shard_map(
        functools.partial(on_device, sizes),
        mesh=mesh,
        in_specs=in_specs,
        out_specs=out_specs,
        check_vma=False,
    )
    if sizes["row"] != sizes["sub"]:
        return step
    return step
```

```python
import functools
import math

import jax
import jax.numpy as jnp
from jax import lax
from jax.experimental import pallas as pl
from jax.experimental.pallas import tpu as pltpu
from jax.sharding import PartitionSpec as P


BLK = 32
OUTER = 2

KAPPA = 40.0
COUPLE = 1.0
EPS = 1e-06
column_block = 2048

F32 = jnp.float32
BF16 = jnp.bfloat16
TILE = 256
CHUNK = 32
ROWS = 2
FEATURES = 96
WAVE = KAPPA / (2.0 * math.pi)
ROUNDER = 12582912.0
HALF_COSINE = (
    0.9999982896004456,
    -4.934458936893249,
    4.048771939331772,
    -1.2478000348360374,
)
LIFT = 256.0
FP8 = jnp.float8_e4m3fn
FP8_PEAK = 224.0


def to_grid(x, step):
    shift = ROUNDER * step
    return (x + shift) - shift


def cos_and_one(turns, amplitude):
    u = turns - jnp.round(turns)
    s = u * u
    factor = math.sqrt(2.0 * amplitude)
    value = HALF_COSINE[-1] * factor
    for coefficient in HALF_COSINE[-2::-1]:
        value = value * s + coefficient * factor
    return value * value


def green(squared_turns):
    y = jnp.maximum(squared_turns, 1e-12)
    turns = y * lax.rsqrt(y)
    amplitude = WAVE * LIFT
    return (cos_and_one(turns, amplitude) - amplitude) / (turns + WAVE)


def features(points):
    row = lax.broadcasted_iota(jnp.int32, points.shape, 0)
    centred = jnp.where(row < 3, (points - 0.5) * WAVE, 0.0)
    high = to_grid(centred, 2.0**-6)
    rest = centred - high
    mid = to_grid(rest, 2.0**-14)
    low = rest - mid
    coarse = jnp.sum(high * high, axis=0, keepdims=True)
    fine = jnp.sum(2.0 * high * rest + rest * rest, axis=0, keepdims=True)
    a = to_grid(coarse, 0.25)
    b = to_grid(coarse - a, 2.0**-10)
    c = coarse - a - b
    d = fine.astype(BF16).astype(F32)
    e = (fine - d).astype(BF16).astype(F32)
    f = fine - d - e
    norm = jnp.zeros_like(centred)
    for k, piece in enumerate((a, b, c, d, e, f)):
        norm = jnp.where(row == k, piece, norm)
    one = jnp.where(row < 6, 1.0, 0.0)
    zero = jnp.zeros_like(centred)
    left = (high, norm, one, high, mid, high, low, mid, mid, low, low, zero)
    right = (high, one, norm, mid, high, low, high, mid, low, mid, low, zero)
    right = tuple(-2.0 * x if k not in (1, 2) else x for k, x in enumerate(right))
    return left, right


def two_pieces(x):
    high = x.astype(BF16).astype(F32)
    return jnp.concatenate([high, x - high], axis=0).astype(BF16)


def fp8_piece(x):
    peak = jnp.maximum(jnp.max(jnp.abs(x), axis=1, keepdims=True), 1e-30)
    return (x * (FP8_PEAK / peak)).astype(FP8), peak * (1.0 / FP8_PEAK)


def nn(left, right):
    return lax.dot_general(left, right, (((1,), (0,)), ((), ())), preferred_element_type=F32)


def nt(left, right):
    return lax.dot_general(left, right, (((1,), (1,)), ((), ())), preferred_element_type=F32)


def prep_kernel(scale, doubled, pack_ref, left_ref, right_ref, field_ref, small_ref, undo_ref):
    pack = pack_ref[...]
    count = pack.shape[1]
    left, right = features(pack[:8])
    right = jnp.concatenate(right, axis=0).astype(BF16)
    weighted = pack[8:] * (pack[3:4] * (scale / LIFT))
    field = two_pieces(weighted)
    small, undo = fp8_piece(weighted)
    undo_ref[...] = jnp.broadcast_to(undo, undo_ref.shape)
    if doubled:
        for k in range(2):
            right_ref[:, k * count : (k + 1) * count] = right
            field_ref[:, k * count : (k + 1) * count] = field
            small_ref[:, k * count : (k + 1) * count] = small
        left = jnp.concatenate(left + (jnp.zeros((128 - FEATURES, count), F32),), axis=0)
        for k in range(count // TILE):
            left_ref[k * TILE : (k + 1) * TILE, :] = left[:, k * TILE : (k + 1) * TILE].T.astype(BF16)
    else:
        half = count // 2
        for k in range(count // TILE):
            to = (k % 2) * half + (k // 2) * TILE
            right_ref[:, to : to + TILE] = right[:, k * TILE : (k + 1) * TILE]
            field_ref[:, to : to + TILE] = field[:, k * TILE : (k + 1) * TILE]
            small_ref[:, to : to + TILE] = small[:, k * TILE : (k + 1) * TILE]


def fill_tile(source, at, target_high, target_low, to):
    for c in range(TILE // CHUNK):
        rows = slice(c * CHUNK, (c + 1) * CHUNK)
        g = green(source[rows, at : at + TILE])
        high = jnp.round(g)
        target_high[rows, to : to + TILE] = high.astype(BF16)
        target_low[rows, to : to + TILE] = (g - high).astype(FP8)


def fold_pieces(x):
    return x[:8] + x[8:]


def build_own_kernel(
    left_ref, right_ref, field_ref, small_ref, undo_ref, high_ref, low_ref, acc_ref, dist
):
    i = pl.program_id(0)
    width = high_ref.shape[1]
    tiles = width // TILE
    here = pl.multiple_of(i * TILE, TILE)

    @pl.when(i == 0)
    def _():
        acc_ref[...] = jnp.zeros_like(acc_ref)

    dist[...] = nn(
        left_ref[pl.ds(here, TILE), :FEATURES], right_ref[:, pl.ds(here, width)]
    )
    mine = field_ref[:, pl.ds(here, TILE)]
    mine_small = small_ref[:, pl.ds(here, TILE)]
    undo = undo_ref[:, :1]
    total = jnp.zeros((8, TILE), F32)
    for k in range(tiles):
        fill_tile(dist, k * TILE, high_ref, low_ref, k * TILE)
        there = pl.ds(pl.multiple_of(here + k * TILE, TILE), TILE)
        high = high_ref[:, k * TILE : (k + 1) * TILE]
        low = low_ref[:, k * TILE : (k + 1) * TILE]
        total += fold_pieces(nt(field_ref[:, there], high)) + nt(small_ref[:, there], low) * undo
        if 0 < k < tiles - 1:
            acc_ref[:, there] += fold_pieces(nn(mine, high)) + nn(mine_small, low) * undo
    acc_ref[:, pl.ds(here, TILE)] += total


def write_partial(part_ref, acc_own, acc_oth):
    count = acc_own.shape[1] // 2
    half = count // 2
    part_ref[:, :count] = acc_own[:, :count] + acc_own[:, count:]
    for b in range(3):
        for k in range(count // TILE):
            at = b * count + (k % 2) * half + (k // 2) * TILE
            to = (b + 1) * count + k * TILE
            part_ref[:, to : to + TILE] = acc_oth[:, at : at + TILE]


def build_oth_kernel(
    parity_ref, left_ref, right_ref, own_ref, own_small_ref, own_undo_ref,
    field_ref, small_ref, undo_ref, acc_in_ref,
    high_ref, low_ref, part_ref, dist, acc_own, acc_oth,
):
    i = pl.program_id(0)
    count = left_ref.shape[0]
    half = count // 2
    tiles = half // TILE
    here = pl.multiple_of(i * TILE, TILE)

    @pl.when(i == 0)
    def _():
        acc_own[...] = acc_in_ref[...]
        acc_oth[...] = jnp.zeros_like(acc_oth)

    offsets = [
        pl.multiple_of(b * count + ((i + parity_ref[b]) & 1) * half, TILE) for b in range(3)
    ]
    left = left_ref[pl.ds(here, TILE), :FEATURES]
    mine = own_ref[:, pl.ds(here, TILE)]
    mine_small = own_small_ref[:, pl.ds(here, TILE)]
    mine_undo = own_undo_ref[:, :1]
    total = jnp.zeros((8, TILE), F32)
    dist[0] = nn(left, right_ref[:, pl.ds(offsets[0], half)])
    for b in range(3):
        if b < 2:
            dist[(b + 1) % 2] = nn(left, right_ref[:, pl.ds(offsets[b + 1], half)])
        undo = undo_ref[:, b * 128 : b * 128 + 1]
        for k in range(tiles):
            to = b * half + k * TILE
            fill_tile(dist.at[b % 2], k * TILE, high_ref, low_ref, to)
            there = pl.ds(pl.multiple_of(offsets[b] + k * TILE, TILE), TILE)
            high = high_ref[:, to : to + TILE]
            low = low_ref[:, to : to + TILE]
            total += fold_pieces(nt(field_ref[:, there], high)) + nt(small_ref[:, there], low) * undo
            acc_oth[:, there] += fold_pieces(nn(mine, high)) + nn(mine_small, low) * mine_undo
    acc_own[:, pl.ds(here, TILE)] += total

    @pl.when(i == pl.num_programs(0) - 1)
    def _():
        write_partial(part_ref, acc_own, acc_oth)


def step_kernel(even_ref, odd_ref, pack_ref, res_ref, *refs):
    cur_ref = refs[0] if len(refs) == 4 else None
    new_res_ref, new_cur_ref, alpha_ref = refs[-3:]
    count = even_ref.shape[1] // 2
    numerator = 0.0
    denominator = 0.0
    for b in range(4):
        source = odd_ref if b % 2 else even_ref
        product = source[:, (b // 2) * count : (b // 2 + 1) * count]
        cols = slice(b * count, (b + 1) * count)
        res = res_ref[:, cols]
        img = pack_ref[4:5, cols] * res + product
        new_res_ref[:, cols] = img
        numerator = numerator + jnp.sum(res * img, axis=1, keepdims=True)
        denominator = denominator + jnp.sum(img * img, axis=1, keepdims=True)
    alpha = numerator / (denominator + EPS)
    alpha_ref[...] = jnp.broadcast_to(alpha, alpha_ref.shape)
    for b in range(4):
        cols = slice(b * count, (b + 1) * count)
        res = res_ref[:, cols]
        if cur_ref is None:
            new_cur_ref[:, cols] = alpha * res
        else:
            new_cur_ref[:, cols] = cur_ref[:, cols] + alpha * res
        new_res_ref[:, cols] = res - alpha * new_res_ref[:, cols]


def apply_kernel(
    scale, parity_ref, pack_ref, res_ref, own_high, own_low, oth_high, oth_low,
    part_ref, own_field, oth_field, own_small, oth_small, undos, acc_own, acc_oth,
):
    i = pl.program_id(0)
    count = res_ref.shape[1] // 4
    half = count // 2

    @pl.when(i == 0)
    def _():
        acc_own[...] = jnp.zeros_like(acc_own)
        acc_oth[...] = jnp.zeros_like(acc_oth)
        for b in range(4):
            cols = slice(b * count, (b + 1) * count)
            weighted = res_ref[:, cols] * (pack_ref[3:4, cols] * (scale / LIFT))
            field = two_pieces(weighted)
            small, undo = fp8_piece(weighted)
            undos[:, b * 128 : (b + 1) * 128] = jnp.broadcast_to(undo, (8, 128))
            if b == 0:
                for k in range(2):
                    own_field[:, k * count : (k + 1) * count] = field
                    own_small[:, k * count : (k + 1) * count] = small
                continue
            for k in range(count // TILE):
                to = (b - 1) * count + (k % 2) * half + (k // 2) * TILE
                oth_field[:, to : to + TILE] = field[:, k * TILE : (k + 1) * TILE]
                oth_small[:, to : to + TILE] = small[:, k * TILE : (k + 1) * TILE]

    width = own_high.shape[1]
    for j in range(ROWS):
        index = i * ROWS + j
        rows = slice(j * TILE, (j + 1) * TILE)
        here = pl.multiple_of(index * TILE, TILE)
        mine = own_field[:, pl.ds(here, TILE)]
        mine_small = own_small[:, pl.ds(here, TILE)]
        undo = undos[:, :1]
        span = pl.ds(here, width)
        inner = pl.ds(pl.multiple_of(here + TILE, TILE), width - 2 * TILE)
        total = fold_pieces(nt(own_field[:, span], own_high[rows, :]))
        total += nt(own_small[:, span], own_low[rows, :]) * undo
        acc_own[:, inner] += (
            fold_pieces(nn(mine, own_high[rows, TILE : width - TILE]))
            + nn(mine_small, own_low[rows, TILE : width - TILE]) * undo
        )
        for b in range(3):
            there = pl.ds(
                pl.multiple_of(b * count + ((index + parity_ref[b]) & 1) * half, TILE), half
            )
            high = oth_high[rows, b * half : (b + 1) * half]
            low = oth_low[rows, b * half : (b + 1) * half]
            total += fold_pieces(nt(oth_field[:, there], high))
            total += nt(oth_small[:, there], low) * undos[:, (b + 1) * 128 : (b + 1) * 128 + 1]
            acc_oth[:, there] += fold_pieces(nn(mine, high)) + nn(mine_small, low) * undo
        acc_own[:, pl.ds(here, TILE)] += total

    @pl.when(i == pl.num_programs(0) - 1)
    def _():
        write_partial(part_ref, acc_own, acc_oth)


def interface_product(field, high, low):
    pieces = two_pieces(field)
    return fold_pieces(nt(pieces, high) + nt(pieces, low))


def couple_kernel(
    source_ref, list_ref, count_ref, first_ref, near_ref, far_ref,
    high_ref, low_ref, weight_ref, out_ref,
):
    count = near_ref.shape[1]
    slots = count_ref.shape[0]
    lane = lax.broadcasted_iota(jnp.int32, (1, count), 1)
    ident = first_ref[0] + lane // BLK
    row = lax.broadcasted_iota(jnp.int32, (128, 128), 0) // BLK
    col = lax.broadcasted_iota(jnp.int32, (128, 128), 1) // BLK
    same = row == col
    for slot in range(slots):
        hits = jnp.zeros((1, count), F32)
        for k in range(list_ref.shape[1]):
            hit = (ident == list_ref[slot, k]) & (k < count_ref[slot])
            hits = hits + jnp.where(hit, 1.0, 0.0)
        weight_ref[slot * 8 : slot * 8 + 8, :] = jnp.broadcast_to(hits, (8, count))
    for g in range(count // 128):
        cols = slice(g * 128, (g + 1) * 128)
        near = near_ref[:8, cols].T
        for slot in range(slots):
            far = far_ref[source_ref[slot], :, cols]
            squared = jnp.zeros((128, 128), F32)
            for x in range(3):
                gap = near[:, x : x + 1] - far[x : x + 1, :]
                squared = squared + gap * gap
            safe = jnp.maximum(squared, 1e-30)
            radius = safe * lax.rsqrt(safe)
            tile = (cos_and_one(radius * WAVE, 1.0) - 1.0) / (1.0 + radius)
            tile = jnp.where(same, tile * (far[3:4, :] * (COUPLE / math.sqrt(BLK))), 0.0)
            high = tile.astype(BF16)
            low = (tile - high.astype(F32)).astype(BF16)
            high_ref[slot, cols, :] = high
            low_ref[slot, cols, :] = low
            rows = slice(slot * 8, slot * 8 + 8)
            out_ref[rows, cols] = interface_product(far[8:], high, low) * weight_ref[rows, cols]


def couple_again_kernel(source_ref, high_ref, low_ref, weight_ref, far_ref, out_ref):
    for g in range(out_ref.shape[1] // 128):
        cols = slice(g * 128, (g + 1) * 128)
        for slot in range(source_ref.shape[0]):
            rows = slice(slot * 8, slot * 8 + 8)
            far = far_ref[source_ref[slot], :, cols]
            product = interface_product(far, high_ref[slot, cols, :], low_ref[slot, cols, :])
            out_ref[rows, cols] = product * weight_ref[rows, cols]


def combine_kernel(source_ref, alpha_ref, first_ref, second_ref, out_ref):
    total = 0.0
    for slot in range(source_ref.shape[0]):
        rows = slice(slot * 8, slot * 8 + 8)
        alpha = alpha_ref[source_ref[slot]]
        total = total + alpha[:8, :1] * first_ref[rows, :] + alpha[8:, :1] * second_ref[rows, :]
    out_ref[...] = total


def whole(shape):
    return pl.BlockSpec(shape, lambda i, *_: (0,) * len(shape))


SMEM = pl.BlockSpec(memory_space=pltpu.SMEM)
VMEM_LIMIT = 48 * 1024 * 1024


def cost(microseconds):
    return pl.CostEstimate(
        flops=int(microseconds * 1e9), bytes_accessed=1000, transcendentals=0
    )


def params(**kw):
    return pltpu.CompilerParams(vmem_limit_bytes=VMEM_LIMIT, **kw)


def on_plane(positions, panel_area, self_term, excitation, adjacency, block_list, block_count):
    count = excitation.shape[2]
    subs = adjacency.shape[0]
    ranks = subs
    unknowns = count * ranks
    scale = 1.0 / math.sqrt(unknowns)
    tiles = count // TILE
    half = count // 2
    own_width = (tiles // 2 + 1) * TILE
    plane = lax.axis_index("row")
    place = lax.axis_index("sub")

    swap = [(z * subs + s, s * subs + z) for z in range(ranks) for s in range(subs)]

    def over(bit):
        return [(s, s ^ bit) for s in range(subs)]

    def send(x, bit):
        return lax.ppermute(x, "sub", over(bit))

    pack = jnp.concatenate(
        [positions[0], panel_area, self_term, jnp.zeros((3, count), F32), excitation[0]],
        axis=0,
    )
    pack = lax.ppermute(pack, ("row", "sub"), swap)

    mine = jnp.arange(subs, dtype=jnp.int32) == plane
    neighbours = jnp.sum(jnp.where(mine[:, None], adjacency, 0), axis=0)
    lists = jnp.sum(jnp.where(mine[:, None, None], block_list, 0), axis=0)
    counts = jnp.sum(jnp.where(mine[:, None], block_count, 0), axis=0)
    source = jnp.maximum((plane - neighbours + subs) % subs - 1, 0)
    first_block = (place * (count // BLK)).astype(jnp.int32).reshape(1)

    def from_planes(x):
        got = []
        for k in range(1, ranks):
            shift = [(z, (z + k) % ranks) for z in range(ranks)]
            got.append(lax.ppermute(x, "row", shift))
        return jnp.stack(got)

    far = from_planes(pack)

    f32 = lambda *s: jax.ShapeDtypeStruct(s, F32)
    b16 = lambda *s: jax.ShapeDtypeStruct(s, BF16)
    fp8 = lambda *s: jax.ShapeDtypeStruct(s, FP8)

    left, right_own, field_own, small_own, undo_own = pl.pallas_call(
        functools.partial(prep_kernel, scale, True),
        out_shape=(
            b16(count, 128),
            b16(FEATURES, 2 * count),
            b16(16, 2 * count),
            fp8(8, 2 * count),
            f32(8, 128),
        ),
        compiler_params=params(),
        name="prep_own",
    )(pack)

    blocks = [pack]
    for bit in range(1, subs):
        blocks.append(send(pack, bit))
    full = jnp.concatenate(blocks, axis=1)

    build_own = pl.pallas_call(
        build_own_kernel,
        grid=(tiles,),
        in_specs=[
            whole((count, 128)),
            whole((FEATURES, 2 * count)),
            whole((16, 2 * count)),
            whole((8, 2 * count)),
            whole((8, 128)),
        ],
        out_specs=(
            pl.BlockSpec((TILE, own_width), lambda i: (i, 0)),
            pl.BlockSpec((TILE, own_width), lambda i: (i, 0)),
            whole((8, 2 * count)),
        ),
        out_shape=(b16(count, own_width), fp8(count, own_width), f32(8, 2 * count)),
        scratch_shapes=[pltpu.VMEM((TILE, own_width), F32)],
        compiler_params=params(),
        cost_estimate=cost(17),
        name="build_own",
    )
    own_high, own_low, acc = build_own(left, right_own, field_own, small_own, undo_own)

    others = []
    for b in range(1, 4):
        others.append(
            pl.pallas_call(
                lambda p, *outs: prep_kernel(scale, False, p, None, *outs),
                out_shape=(b16(FEATURES, count), b16(16, count), fp8(8, count), f32(8, 128)),
                compiler_params=params(),
                name="prep_oth",
            )(blocks[b])
        )
    right_oth, field_oth, small_oth, undo_oth = (
        jnp.concatenate(parts, axis=1) for parts in zip(*others)
    )

    parity = jnp.stack([(place > (place ^ b)).astype(jnp.int32) for b in range(1, 4)])

    build_oth = pl.pallas_call(
        build_oth_kernel,
        grid_spec=pltpu.PrefetchScalarGridSpec(
            num_scalar_prefetch=1,
            grid=(tiles,),
            in_specs=[
                whole((count, 128)),
                whole((FEATURES, 3 * count)),
                whole((16, 2 * count)),
                whole((8, 2 * count)),
                whole((8, 128)),
                whole((16, 3 * count)),
                whole((8, 3 * count)),
                whole((8, 3 * 128)),
                whole((8, 2 * count)),
            ],
            out_specs=(
                pl.BlockSpec((TILE, 3 * half), lambda i, *_: (i, 0)),
                pl.BlockSpec((TILE, 3 * half), lambda i, *_: (i, 0)),
                whole((8, 4 * count)),
            ),
            scratch_shapes=[
                pltpu.VMEM((2, TILE, half), F32),
                pltpu.VMEM((8, 2 * count), F32),
                pltpu.VMEM((8, 3 * count), F32),
            ],
        ),
        out_shape=(b16(count, 3 * half), fp8(count, 3 * half), f32(8, 4 * count)),
        compiler_params=params(),
        cost_estimate=cost(42),
        name="build_oth",
    )
    oth_high, oth_low, part = build_oth(
        parity, left, right_oth, field_own, small_own, undo_own,
        field_oth, small_oth, undo_oth, acc,
    )

    def pair(x, a, b):
        return jnp.concatenate(
            [x[:, a * count : (a + 1) * count], x[:, b * count : (b + 1) * count]], axis=1
        )

    def reduce_all(part):
        got = send(pair(part, 1, 3), 1)
        chip = pair(part, 0, 2) + got
        got = send(chip, 2)
        even = chip + pair(got, 1, 0)
        odd = send(even, 1)
        return even, odd

    def apply(res):
        own_spec = pl.BlockSpec((ROWS * TILE, own_width), lambda i, *_: (i, 0))
        oth_spec = pl.BlockSpec((ROWS * TILE, 3 * half), lambda i, *_: (i, 0))
        return pl.pallas_call(
            functools.partial(apply_kernel, scale),
            grid_spec=pltpu.PrefetchScalarGridSpec(
                num_scalar_prefetch=1,
                grid=(tiles // ROWS,),
                in_specs=[
                    whole((16, 4 * count)),
                    whole((8, 4 * count)),
                    own_spec,
                    own_spec,
                    oth_spec,
                    oth_spec,
                ],
                out_specs=whole((8, 4 * count)),
                scratch_shapes=[
                    pltpu.VMEM((16, 2 * count), BF16),
                    pltpu.VMEM((16, 3 * count), BF16),
                    pltpu.VMEM((8, 2 * count), FP8),
                    pltpu.VMEM((8, 3 * count), FP8),
                    pltpu.VMEM((8, 4 * 128), F32),
                    pltpu.VMEM((8, 2 * count), F32),
                    pltpu.VMEM((8, 3 * count), F32),
                ],
            ),
            out_shape=f32(8, 4 * count),
            compiler_params=params(),
            cost_estimate=cost(22),
            name="apply",
        )(parity, full, res, own_high, own_low, oth_high, oth_low)

    def step(part, res, *cur):
        even, odd = reduce_all(part)
        return pl.pallas_call(
            step_kernel,
            out_shape=[f32(8, 4 * count)] * 2 + [f32(8, 128)],
            compiler_params=params(),
            name="step",
        )(even, odd, full, res, *cur)

    slots = adjacency.shape[1]
    vmem = pl.BlockSpec(memory_space=pltpu.VMEM)
    interface = pl.pallas_call(
        couple_kernel,
        in_specs=[SMEM] * 4 + [vmem] * 2,
        out_shape=(
            b16(slots, count, 128),
            b16(slots, count, 128),
            f32(8 * slots, count),
            f32(8 * slots, count),
        ),
        compiler_params=params(),
        cost_estimate=cost(4),
        name="couple",
    )
    tile_high, tile_low, weight, first_part = interface(
        source, lists, counts, first_block, pack, far
    )

    res, cur, alpha_first = step(part, full[8:])
    far_res = from_planes(res[:, :count])
    part = apply(res)
    second_part = pl.pallas_call(
        couple_again_kernel,
        in_specs=[SMEM] + [vmem] * 4,
        out_shape=f32(8 * slots, count),
        compiler_params=params(),
        cost_estimate=cost(1),
        name="couple_again",
    )(source, tile_high, tile_low, weight, far_res)
    res, cur, alpha_second = step(part, res, cur)
    coupled = pl.pallas_call(
        combine_kernel,
        in_specs=[SMEM] + [vmem] * 3,
        out_shape=f32(8, count),
        compiler_params=params(),
        name="combine",
    )(
        source,
        from_planes(jnp.concatenate([alpha_first, alpha_second], axis=0)),
        first_part,
        second_part,
    )
    res = res - jnp.concatenate(
        [coupled] + [send(coupled, bit) for bit in range(1, subs)], axis=1
    )

    res, cur, _ = step(apply(res), res, cur)
    res, cur, _ = step(apply(res), res, cur)
    out = jnp.concatenate([cur[:, :count], res[:, :count]], axis=0)
    out = lax.ppermute(out, ("row", "sub"), swap)
    return out[None, :8], out[None, 8:]


def kernel_tile(near, far, area, scale):
    squared = jnp.zeros(near.shape[1:] + far.shape[-1:], jnp.float32)
    for coord in range(3):
        spacing = near[coord][..., :, None] - far[coord][..., None, :]
        squared = squared + spacing * spacing
    radius = jnp.sqrt(squared)
    return jnp.cos(KAPPA * radius) / (1.0 + radius) * (area * scale)[..., None, :]


def pick_source(table, chosen):
    shaped = chosen.reshape(chosen.shape + (1,) * (table.ndim - 1))
    return jnp.sum(jnp.where(shaped, table, jnp.zeros_like(table)), axis=0)


def on_rows(positions, panel_area, self_term, excitation, adjacency, block_list, block_count):
    width = excitation.shape[1]
    rows_here = excitation.shape[2]
    near = positions[0]
    diagonal = self_term[0]
    gathered_pos, gathered_area = (
        lax.all_gather(positions[0], "row", axis=1, tiled=True),
        lax.all_gather(panel_area[0], "row", axis=0, tiled=True),
    )
    other_pos, other_area = (
        lax.all_gather(positions, "sub", axis=0, tiled=True),
        lax.all_gather(panel_area, "sub", axis=0, tiled=True),
    )
    total_cols = gathered_pos.shape[1]
    scale = 1.0 / math.sqrt(total_cols)
    subdomains = adjacency.shape[0]
    local_blocks = rows_here // BLK

    def build_step(counter, stored):
        offset = counter * column_block
        block_pos = lax.dynamic_slice_in_dim(gathered_pos, offset, column_block, 1)
        block_area = lax.dynamic_slice_in_dim(gathered_area, offset, column_block, 0)
        tile = kernel_tile(near, block_pos, block_area, scale)
        return lax.dynamic_update_slice_in_dim(stored, tile, offset, 1)

    self_rows = lax.fori_loop(
        0, total_cols // column_block, build_step, jnp.zeros((rows_here, total_cols), jnp.float32)
    )

    def apply_self(field):
        product = lax.dot_general(
            lax.all_gather(field[None], "row", axis=2, tiled=True)[0],
            self_rows,
            (((1,), (1,)), ((), ())),
            precision=lax.Precision.HIGHEST,
            preferred_element_type=jnp.float32,
        )
        return diagonal[None, :] * field + product

    currents = jnp.zeros((width, rows_here), jnp.float32)
    residual = excitation[0]
    for outer_step in range(OUTER):
        if outer_step > 0:
            all_currents = lax.all_gather(currents[None], "sub", axis=0, tiled=True)
            mine = jnp.arange(subdomains, dtype=jnp.int32) == lax.axis_index("sub")
            my_adjacency = jnp.sum(jnp.where(mine[:, None], adjacency, 0), axis=0)
            my_lists = jnp.sum(jnp.where(mine[:, None, None], block_list, 0), axis=0)
            my_counts = jnp.sum(jnp.where(mine[:, None], block_count, 0), axis=0)
            first_block = lax.axis_index("row") * local_blocks
            global_ids = first_block + jnp.arange(local_blocks, dtype=jnp.int32)
            total = jnp.zeros((width, local_blocks, BLK), jnp.float32)
            for slot in range(adjacency.shape[1]):
                chosen = jnp.arange(subdomains, dtype=jnp.int32) == my_adjacency[slot]
                src_pos = pick_source(other_pos, chosen)
                src_area = pick_source(other_area, chosen)
                src_cur = pick_source(all_currents, chosen)
                tiles = kernel_tile(
                    near.reshape(3, local_blocks, BLK),
                    src_pos.reshape(3, local_blocks, BLK),
                    src_area.reshape(local_blocks, BLK),
                    COUPLE / math.sqrt(BLK),
                )
                coupling_product = jnp.einsum(
                    "bpq,ebq->ebp",
                    tiles,
                    src_cur.reshape(width, local_blocks, BLK),
                    precision=lax.Precision.HIGHEST,
                )
                listed = (my_lists[slot][:, None] == global_ids[None, :]) & (
                    jnp.arange(my_lists.shape[1], dtype=jnp.int32)[:, None] < my_counts[slot]
                )
                weight = jnp.sum(listed.astype(jnp.float32), axis=0)
                total = total + coupling_product * weight[None, :, None]
            coupled = total.reshape(width, rows_here)
            residual = residual - coupled
        image = apply_self(residual)
        second = apply_self(image)
        cross, square, res_second, img_second, sec_second = lax.psum(
            (
                jnp.sum(residual * image, axis=1),
                jnp.sum(image * image, axis=1),
                jnp.sum(residual * second, axis=1),
                jnp.sum(image * second, axis=1),
                jnp.sum(second * second, axis=1),
            ),
            "row",
        )
        first_alpha = cross / (square + EPS)
        currents = currents + first_alpha[:, None] * residual
        residual = residual - first_alpha[:, None] * image
        image = image - first_alpha[:, None] * second
        cross_next = (
            cross
            - first_alpha * res_second
            - first_alpha * square
            + first_alpha * first_alpha * img_second
        )
        square_next = (
            square - 2.0 * first_alpha * img_second + first_alpha * first_alpha * sec_second
        )
        next_alpha = cross_next / (square_next + EPS)
        currents = currents + next_alpha[:, None] * residual
        residual = residual - next_alpha[:, None] * image
    return (currents[None], residual[None])


def on_device(sizes, *arrays):
    excitation, adjacency = arrays[3], arrays[4]
    count = excitation.shape[2]
    square = sizes["row"] == sizes["sub"] == adjacency.shape[0] == 4
    if square and excitation.shape[1] == 8 and count % (2 * TILE) == 0:
        return on_plane(*arrays)
    return on_rows(*arrays)


def solution(mesh):
    in_specs = (
        P(("body", "sub"), None, "row"),
        P(("body", "sub"), "row"),
        P(("body", "sub"), "row"),
        P(("body", "sub"), None, "row"),
        P("body", None),
        P("body", None, None),
        P("body", None),
    )
    out_specs = (P(("body", "sub"), None, "row"), P(("body", "sub"), None, "row"))
    sizes = {name: mesh.shape[name] for name in ("row", "sub")}
    step = jax.shard_map(
        functools.partial(on_device, sizes),
        mesh=mesh,
        in_specs=in_specs,
        out_specs=out_specs,
        check_vma=False,
    )
    if sizes["row"] != sizes["sub"]:
        return step
    return step
```
